256 devices in a mesh: prow: 32 (over x, z), pcol: 8 (over y, core).
Axes of the slice: x: 4, y: 4, z: 8, core: 2. Of those that a mesh axis runs over, the one named last changes fastest.
Arguments:
- anc_inverse: bfloat16 [4, 32, 256, 16, 8, 256], P(None, 'prow', None, None, 'pcol'), may hold values from -6 to 6
- first_lower: bfloat16 [4, 32, 256, 256], P(None, 'prow', 'pcol'), may hold values from -0.046875 to 0.046875
- second_lower: bfloat16 [4, 32, 256, 256], P(None, 'prow', 'pcol'), may hold values from -0.0546875 to 0.0546875
- second_top: bfloat16 [256, 256], replicated, may hold values from -0.3125 to 0.3125
- struct_first: int32 [128], replicated, may hold values from 0 to 1
- struct_keep: int32 [128], replicated, may hold values from 0 to 1
- pivot_h: float32 [2, 256, 256], replicated, as said below
- pivot_s: float32 [2, 256, 256], replicated, as said below
- shifts: float32 [40], replicated, may hold values from 0.5 to 4
- pole_index: int32 [40], replicated, may hold values from 0 to 39, each once
Outputs:
- first_column: bfloat16 [4, 32, 256, 256], P(None, 'prow', 'pcol')
- first_diag: float32 [256, 256], replicated
- link_column: bfloat16 [256, 256], replicated
- second_column: bfloat16 [4, 32, 256, 256], P(None, 'prow', 'pcol')
- second_diag: float32 [256, 256], replicated
The draws below stay inside these ranges and needn't reach their ends.
Inputs may be any that keep to these rules, and one draw needn't show every extreme that they name: `struct_first`: 1 marks a block row of the first supernode's structure. `struct_keep`: 1 marks a structure block that the second supernode keeps. `pole_index`: each pole appears once. `pivot_h`: symmetric, with a positive diagonal larger than each row's off-diagonal magnitudes together. `pivot_s`: symmetric, with a positive diagonal larger than each row's off-diagonal magnitudes together.
All inputs are finite; a program needn't handle non-finite values.
Results may differ from the reference program's by a relative error of at most 0.0041.
The reference program's roundings to bfloat16 on the way count: a program that leaves them out, or rounds other values in their place, can miss the bound.
Values may be sent and summed in bfloat16 or wider, within the bound.
A program may use at most 64 MiB of HBM per device.

```python
import math
import jax
import jax.numpy as jnp
from jax import lax

W = 256
RB = 4
NPOLE = 40
NBA = 128
CB = 16
N_PROW = 32
N_PCOL = 8


def pivot_single(key, overall):
    off_key = jax.random.fold_in(key, 101)
    diag_key = jax.random.fold_in(key, 202)
    coupling_key = jax.random.fold_in(key, 303)
    sign_key = jax.random.fold_in(key, 404)
    base = jax.random.uniform(off_key, (W, W), jnp.float32, -0.05 / W, 0.05 / W)
    symmetric = (base + base.T) * 0.5
    identity = jnp.eye(W, dtype=jnp.float32)
    dense = symmetric * (1.0 - identity)
    diagonal = jax.random.uniform(diag_key, (W,), jnp.float32, 1.0, 2.0)
    smaller = jnp.minimum(diagonal[:-1], diagonal[1:])
    strength = jax.random.uniform(coupling_key, (W - 1,), jnp.float32, 0.3, 0.45)
    coin = jax.random.uniform(sign_key, (W - 1,), jnp.float32, 0.0, 1.0)
    signs = jnp.where(coin < 0.5, -1.0, 1.0).astype(jnp.float32)
    neighbour = strength * smaller * signs
    banded = jnp.diag(neighbour, 1) + jnp.diag(neighbour, -1)
    return (dense + banded + identity * diagonal[:, None]) * overall


def pivot_block(key, overall):
    first = pivot_single(jax.random.fold_in(key, 1), overall)
    second = pivot_single(jax.random.fold_in(key, 2), overall)
    return jnp.stack([first, second], axis=0)


def draw_pivot_h(key, part):
    return pivot_block(jax.random.fold_in(key, 11), 1.0)


def draw_pivot_s(key, part):
    return pivot_block(jax.random.fold_in(key, 23), 0.25)


def set_ends(entries, rng, smallest, largest):
    longest = entries.shape.index(max(entries.shape))
    spots = []
    for shift in (0, 1):
        where = [jax.random.randint(jax.random.fold_in(rng, axis), (), 0, length) for axis, length in enumerate(entries.shape)]
        where[longest] = (where[longest] + shift) % entries.shape[longest]
        spots.append(tuple(where))
    return entries.at[spots[0]].set(smallest).at[spots[1]].set(largest)


def block_levels(rng, dims, split, low, high):
    def one(axis_at, parts):
        steps = jax.random.uniform(jax.random.fold_in(jax.random.fold_in(rng, 6), axis_at), (parts,), jnp.float32, low / len(split), high / len(split))
        return jnp.repeat(jnp.exp(steps), dims[axis_at] // parts).reshape((-1,) + (1,) * (len(dims) - axis_at - 1))

    level = one(*split[0])
    for cut in split[1:]:
        level = level * one(*cut)
    return level


def gaussian(rng, extent, width, most, cuts=(), kind=jnp.bfloat16):
    level = block_levels(rng, extent, cuts, -0.22, 0.18) if cuts else 1.0
    values = jax.random.normal(rng, extent, jnp.float32) * width * level
    return jnp.minimum(jnp.maximum(values, -most), most).astype(kind)


def setup_inputs(seed: int = 0) -> dict:
    key_list = jax.random.split(jax.random.key(seed), 11)
    return {
        "anc_inverse": gaussian(key_list[0], (RB, N_PROW, W, CB, N_PCOL, W), 1.0, 6.0, ((1, 32), (4, 8))),
        "first_lower": gaussian(key_list[1], (RB, N_PROW, W, W), (NBA * W // 2) ** -0.5, 0.046875, ((1, 32), (2, 8))),
        "second_lower": gaussian(key_list[2], (RB, N_PROW, W, W), (NBA * W // 3) ** -0.5, 0.0546875, ((1, 32), (2, 8))),
        "second_top": gaussian(key_list[3], (W, W), 0.02, 0.3125),
        "struct_first": set_ends(jax.random.randint(key_list[4], (NBA,), 0, 2), jax.random.fold_in(key_list[4], 1), 0, 1).astype(jnp.int32),
        "struct_keep": set_ends(jax.random.randint(key_list[5], (NBA,), 0, 2), jax.random.fold_in(key_list[5], 1), 0, 1).astype(jnp.int32),
        "pivot_h": draw_pivot_h(jax.random.fold_in(key_list[10], 71), 0),
        "pivot_s": draw_pivot_s(jax.random.fold_in(key_list[10], 71), 0),
        "shifts": jnp.clip(jnp.exp(jax.random.uniform(key_list[8], (NPOLE,), jnp.float32, math.log(0.5), math.log(4.0))), 0.5, 4.0),
        "pole_index": jax.random.permutation(key_list[9], NPOLE).astype(jnp.int32),
    }


def pivot_inverse(h_block, s_block, shift):
    factor = jnp.linalg.cholesky(h_block + shift * s_block)
    identity = jnp.eye(h_block.shape[0], dtype=jnp.float32)
    return jax.scipy.linalg.cho_solve((factor, True), identity)

def reference(anc_inverse, first_lower, second_lower, second_top, struct_first, struct_keep, pivot_h, pivot_s, shifts, pole_index):
    blocks = RB * N_PROW
    order = blocks * W
    first_mask = struct_first.astype(jnp.float32)
    second_mask = first_mask * struct_keep.astype(jnp.float32)
    row_first = jnp.repeat(first_mask, W)
    row_second = jnp.repeat(second_mask, W)
    lower_first = first_lower.reshape(order, W) * row_first.astype(jnp.bfloat16)[:, None]
    lower_second = second_lower.reshape(order, W) * row_second.astype(jnp.bfloat16)[:, None]
    stacked = jnp.concatenate([lower_first, lower_second], axis=1).astype(jnp.float32)
    whole = anc_inverse.reshape(blocks, W, order)

    def block_row(rows):
        return jnp.dot(rows.astype(jnp.float32), stacked, precision=lax.Precision.HIGHEST)
    product = lax.map(block_row, whole).reshape(order, 2 * W)
    first_col = (-product[:, :W] * row_first[:, None]).astype(jnp.bfloat16)
    bridge = jnp.dot(first_col.astype(jnp.float32), second_top.astype(jnp.float32), preferred_element_type=jnp.float32)
    second_col = (-(product[:, W:] + bridge) * row_second[:, None]).astype(jnp.bfloat16)
    shift = shifts[pole_index[0]]
    first_diag = pivot_inverse(pivot_h[0], pivot_s[0], shift) - jnp.dot(lower_first.T.astype(jnp.float32), first_col.astype(jnp.float32), preferred_element_type=jnp.float32)
    cross = jnp.dot(first_col.T.astype(jnp.float32), lower_second.astype(jnp.float32), preferred_element_type=jnp.float32)
    link_col = (-(cross + jnp.dot(first_diag.astype(jnp.bfloat16).astype(jnp.float32), second_top.astype(jnp.float32), preferred_element_type=jnp.float32))).astype(jnp.bfloat16)
    second_diag = pivot_inverse(pivot_h[1], pivot_s[1], shift) - jnp.dot(lower_second.T.astype(jnp.float32), second_col.astype(jnp.float32), preferred_element_type=jnp.float32) - jnp.dot(second_top.T.astype(jnp.float32), link_col.astype(jnp.float32), preferred_element_type=jnp.float32)
    return (first_col.reshape(RB, N_PROW, W, W), first_diag, link_col, second_col.reshape(RB, N_PROW, W, W), second_diag)
```

```python
import jax
import jax.numpy as jnp
from jax import lax
from jax.experimental import pallas as pl
from jax.experimental.pallas import tpu as pltpu
from jax.sharding import PartitionSpec as P

MESH = pl.DeviceIdType.MESH
F32 = jnp.float32
BF16 = jnp.bfloat16
HI = lax.Precision.HIGHEST
NX, NZ, NY = 4, 8, 4
W = 256
BLK = 32


def sweep_block(x):
    n = x.shape[0]
    rows = lax.broadcasted_iota(jnp.int32, (n, n), 0)
    cols = lax.broadcasted_iota(jnp.int32, (n, n), 1)
    row1 = lax.broadcasted_iota(jnp.int32, (n, 1), 0)
    col1 = lax.broadcasted_iota(jnp.int32, (1, n), 1)
    for k in range(n):
        inv = 1.0 / x[k : k + 1, k : k + 1]
        right = jnp.where(col1 == k, 1.0, x[k : k + 1, :]) * inv
        left = jnp.where(row1 == k, 1.0, -x[:, k : k + 1])
        x = jnp.where((rows == k) | (cols == k), 0.0, x) + left * right
    return x


def body(
    anc,
    l1,
    l2,
    top,
    keep1,
    keep2,
    piv_h,
    piv_s,
    shifts,
    pole,
    fc_out,
    fd_out,
    link_out,
    sc_out,
    sd_out,
    abuf,
    a32,
    abf,
    m,
    lm,
    prod,
    r1,
    r2,
    g,
    gs,
    terms,
    w1,
    u,
    w2,
    w3,
    w4,
    wf,
    load_sem,
    sc_s,
    sc_r,
    sc_l,
    a1_s,
    a1_r,
    a2_s,
    a2_r,
    b1_s,
    b1_r,
    b2_s,
    b2_r,
    b3_s,
    b3_r,
    r1_s,
    r1_r,
    r2_s,
    r2_r,
    p1_s,
    p1_r,
    p2_s,
    p2_r,
    p3_s,
    p3_r,
    p4_s,
    p4_r,
    p5_s,
    p5_r,
):
    prow = lax.axis_index("prow")
    q = lax.axis_index("pcol")
    x, z = prow // NZ, prow % NZ
    y, core = q // 2, q % 2

    def dev(xx, zz, qq):
        return {"prow": xx * NZ + zz, "pcol": qq}

    def xr(d):
        return (x + d) % NX

    def zr(d):
        return (z + d) % NZ

    def remote(src, dst, ssem, rsem, target):
        return pltpu.make_async_remote_copy(
            src_ref=src, dst_ref=dst, send_sem=ssem, recv_sem=rsem, device_id=target, device_id_type=MESH
        )

    sent = []

    def send(src, dst, ssem, rsem, target):
        copy = remote(src, dst, ssem, rsem, target)
        copy.start()
        sent.append(copy)

    def arrived(dst, ssem, rsem):
        remote(dst, dst, ssem, rsem, dev(x, z, (q + 1) % 8)).wait_recv()

    loads = [pltpu.make_async_copy(piv_h.at[core], g, load_sem.at[4])]
    loads.append(pltpu.make_async_copy(piv_s.at[core], gs, load_sem.at[5]))
    for a in range(4):
        loads.append(pltpu.make_async_copy(anc.at[a], abuf.at[a], load_sem.at[a]))
    for copy in loads:
        copy.start()

    barrier = pltpu.get_barrier_semaphore()

    def greet(target):
        pl.semaphore_signal(barrier, inc=1, device_id=target, device_id_type=MESH)

    @pl.when(q != z)
    def _():
        for d in range(8):
            greet(dev(x, q, d))

    for d in range(1, 8):
        greet(dev(x, z, (q + d) % 8))
        greet(dev(x, zr(d), q))
    for d in range(1, 4):
        greet(dev(xr(d), z, q))

    flag1 = [keep1[a * (NX * NZ) + prow].astype(F32) for a in range(4)]
    flag2 = [flag1[a] * keep2[a * (NX * NZ) + prow].astype(F32) for a in range(4)]
    for a in range(4):
        lm[0, a] = (l1[a].astype(F32) * flag1[a]).astype(BF16).reshape(2, 16, W)
        lm[1, a] = (l2[a].astype(F32) * flag2[a]).astype(BF16).reshape(2, 16, W)

    pl.semaphore_wait(barrier, 24)

    for h in range(2):

        def whole(d, h=h):
            zz = zr(d)
            src = lm.at[h, zz // 2, zz % 2]
            dst = m.at[h, zz // 2, x, q, zz % 2]
            return remote(src, dst, sc_s.at[h, d], sc_r.at[h, q], dev(x, zz, z))

        @pl.when(q == z)
        def _(h=h):
            pltpu.make_async_copy(
                lm.at[h, z // 2, z % 2], m.at[h, z // 2, x, q, z % 2], sc_l.at[h]
            ).start()

        @pl.when(q != z)
        def _(whole=whole):
            whole(0).start()

        for d in range(1, 8):
            whole(d).start()

    def relayout(a):
        loads[2 + a].wait()

        def widen(i, _):
            rows = pl.ds(pl.multiple_of(i * 512, 512), 512)
            for s in range(2):
                a32[s, rows, :] = abuf[a, rows, s * 128 : (s + 1) * 128].astype(F32)
            return 0

        lax.fori_loop(0, 8, widen, 0)
        for c in range(16):
            for s in range(2):
                lanes = slice(c * W + s * 128, c * W + (s + 1) * 128)
                abf[a * W : (a + 1) * W, lanes] = a32[s, pl.ds(c, W, stride=16), :].astype(BF16)

    relayout(0)
    loads[0].wait()
    loads[1].wait()
    shift = shifts[pole[0]]
    g[...] = g[...] + shift * gs[...]

    def invert_step(k):
        rows = pl.ds(pl.multiple_of(k * BLK, BLK), BLK)
        panel = g[rows, :]
        unit = (
            lax.broadcasted_iota(jnp.int32, (BLK, W), 1)
            == lax.broadcasted_iota(jnp.int32, (BLK, W), 0) + k * BLK
        ).astype(F32)
        lanes = lax.broadcasted_iota(jnp.int32, (BLK, W), 1)
        inside = (lanes >= k * BLK) & (lanes < k * BLK + BLK)
        pivot = lax.dot_general(
            panel, unit, (((1,), (1,)), ((), ())), precision=HI, preferred_element_type=F32
        )
        solved = jnp.dot(
            sweep_block(pivot), jnp.where(inside, -unit, panel), precision=HI, preferred_element_type=F32
        )
        g[...] = g[...] - lax.dot_general(
            panel, solved + unit, (((0,), (0,)), ((), ())), precision=HI, preferred_element_type=F32
        )
        g[rows, :] = solved

    def invert(first, last):
        def step(k, _):
            invert_step(k)
            return 0

        lax.fori_loop(first, last, step, 0)

    lo, hi = pl.ds(0, 4), pl.ds(4, 4)

    def mine(h, zz, part):
        return m.at[h, zz // 2, x, part, zz % 2]

    def group(h, zz, s):
        return m.at[h, zz // 2, pl.ds(2 * s, 2), lo, zz % 2]

    def at_x(h, zz, xx):
        return m.at[h, zz // 2, xx, hi, zz % 2]

    def cross(h, d):
        zz = zr(d)
        send(mine(h, zz, hi), mine(h, zz, hi), b2_s.at[h, d % 8, 0], b2_r.at[h, d % 8, 0], dev(xr(1), z, q))
        send(mine(h, zz, hi), mine(h, zz, hi), b2_s.at[h, d % 8, 1], b2_r.at[h, d % 8, 1], dev(xr(3), z, q))

    def high_z(h, r):
        for i, step in enumerate((1, -1)):
            zz = zr(-step * (r - 1))
            if r < 4:
                part = hi
            else:
                part = pl.ds(4 + 2 * i, 2)
            ref = mine(h, zz, part)
            send(ref, ref, b1_s.at[h, r - 1, i], b1_r.at[h, r - 1, i], dev(x, zr(step), q))

    def high_z_wait(h, r):
        for i, step in enumerate((1, -1)):
            zz = zr(-step * r)
            part = hi if r < 4 else pl.ds(4 + 2 * i, 2)
            arrived(mine(h, zz, part), b1_s.at[h, r - 1, i], b1_r.at[h, r - 1, i])

    def low_z(h, r, s):
        for i, step in enumerate((1, -1)):
            if r == 4 and s != i:
                continue
            ref = group(h, zr(-step * (r - 1)), s)
            send(ref, ref, a2_s.at[h, r - 1, i, s], a2_r.at[h, r - 1, i, s], dev(x, zr(step), q))

    def low_z_wait(h, r, s):
        for i, step in enumerate((1, -1)):
            if r == 4 and s != i:
                continue
            arrived(group(h, zr(-step * r), s), a2_s.at[h, r - 1, i, s], a2_r.at[h, r - 1, i, s])

    def start(h):
        @pl.when(q == z)
        def _():
            pltpu.make_async_copy(
                lm.at[h, z // 2, z % 2], m.at[h, z // 2, x, q, z % 2], sc_l.at[h]
            ).wait()

        for d in range(8):
            src_q = (q + d) % 8
            dst = m.at[h, z // 2, x, src_q, z % 2]
            if d == 0:

                @pl.when(q != z)
                def _(dst=dst, src_q=src_q):
                    arrived(dst, sc_s.at[h, 0], sc_r.at[h, src_q])
            else:
                arrived(dst, sc_s.at[h, d], sc_r.at[h, src_q])
        for d in (1, 3, 2):
            ref = mine(h, z, lo)
            send(ref, ref, a1_s.at[h, d - 1], a1_r.at[h, d - 1], dev(xr(d), z, q))
        high_z(h, 1)
        cross(h, 0)

    def low_start(h):
        for d in (1, 3, 2):
            arrived(m.at[h, z // 2, xr(-d), lo, z % 2], a1_s.at[h, d - 1], a1_r.at[h, d - 1])
        for s in range(2):
            low_z(h, 1, s)

    def low(h, r):
        for s in range(2):
            low_z_wait(h, r, s)
            if r < 4:
                low_z(h, r + 1, s)

    def high(h, r):
        high_z_wait(h, r)
        if r < 4:
            high_z(h, r + 1)
            cross(h, r)
            cross(h, -r)
        else:
            cross(h, 4)

    def hop(h, d):
        zz = zr(d)
        slot = d % 8
        arrived(at_x(h, zz, xr(-1)), b2_s.at[h, slot, 0], b2_r.at[h, slot, 0])
        arrived(at_x(h, zz, xr(1)), b2_s.at[h, slot, 1], b2_r.at[h, slot, 1])
        if d in (0, 1, 2, -3):
            ref = at_x(h, zz, xr(-1))
            send(ref, ref, b3_s.at[h, slot], b3_r.at[h, slot], dev(xr(1), z, q))
        else:
            ref = at_x(h, zz, xr(1))
            send(ref, ref, b3_s.at[h, slot], b3_r.at[h, slot], dev(xr(3), z, q))

    def hop_wait(h):
        for d in range(8):
            arrived(at_x(h, zr(d), xr(2)), b3_s.at[h, d], b3_r.at[h, d])

    def multiply(h):
        def rows(a, _):
            weights = m[h].reshape(16 * W, W)
            part = jnp.dot(
                abf[pl.ds(pl.multiple_of(a * W, W), W), :], weights, preferred_element_type=F32
            )
            prod[h, a] = part.reshape(4, 2, 32, W)
            remote(
                prod.at[h, a, :, 1 - core],
                r1.at[h, a],
                r1_s.at[h, a],
                r1_r.at[h, a],
                dev(x, z, q + 1 - 2 * core),
            ).start()
            return 0

        lax.fori_loop(0, 4, rows, 0)

    def pair_sum(h):
        def rows(a, _):
            remote(
                prod.at[h, a, :, 1 - core],
                r1.at[h, a],
                r1_s.at[h, a],
                r1_r.at[h, a],
                dev(x, z, q + 1 - 2 * core),
            ).wait_recv()
            for yy in range(4):
                prod[h, a, yy, core] = prod[h, a, yy, core] + r1[h, a, yy]
            for d in (2, 1, 3):
                yy = (y + d) % NY
                remote(
                    prod.at[h, a, yy, core],
                    r2.at[h, d - 1, a],
                    r2_s.at[h, d - 1, a],
                    r2_r.at[h, d - 1, a],
                    dev(x, z, yy * 2 + core),
                ).start()
            return 0

        lax.fori_loop(0, 4, rows, 0)

    def y_copy(h, d, a):
        yy = (y + d) % NY
        return remote(
            prod.at[h, a, yy, core],
            r2.at[h, d - 1, a],
            r2_s.at[h, d - 1, a],
            r2_r.at[h, d - 1, a],
            dev(x, z, yy * 2 + core),
        )

    def row_part(h, a):
        total = prod[h, a, y, core]
        for d in (1, 2, 3):
            y_copy(h, d, a).wait_recv()
            total = total + r2[h, d - 1, a]
        return total

    def finish_first():
        for a in range(4):
            fc_out[a] = (-row_part(0, a) * flag1[a]).astype(BF16)

    def finish_second():
        for a in range(4):
            bridge = jnp.dot(fc_out[a], top[...], preferred_element_type=F32)
            sc_out[a] = (-(row_part(1, a) + bridge) * flag2[a]).astype(BF16)

    start(0)
    low_start(0)
    high(0, 1)
    relayout(1)
    high(0, 2)
    start(1)
    low(0, 1)
    high(0, 3)
    hop(0, 0)
    high(0, 4)
    hop(0, 1)
    hop(0, -1)
    relayout(2)
    low(0, 2)
    low_start(1)
    high(1, 1)
    hop(0, 2)
    hop(0, -2)
    high(1, 2)
    relayout(3)
    low(0, 3)
    hop(0, 3)
    hop(0, -3)
    hop(0, 4)
    high(1, 3)
    low(0, 4)
    low(1, 1)
    high(1, 4)
    hop_wait(0)
    multiply(0)
    for d in (0, 1, -1, 2, -2):
        hop(1, d)
    low(1, 2)
    pair_sum(0)
    for d in (3, -3, 4):
        hop(1, d)
    invert(0, 1)
    low(1, 3)
    finish_first()
    invert(1, 2)
    low(1, 4)
    hop_wait(1)
    multiply(1)
    pair_sum(1)
    invert(2, 8)
    finish_second()

    def contract(left, right):
        return lax.dot_general(left, right, (((0,), (0,)), ((), ())), preferred_element_type=F32)

    lower1 = lm[0].reshape(128, W)
    lower2 = lm[1].reshape(128, W)
    first = fc_out[...].reshape(128, W)
    second = sc_out[...].reshape(128, W)
    owner1 = ((prow == 0) & (q == 0)).astype(F32)
    owner2 = ((prow == 0) & (q == 1)).astype(F32)
    terms[:, 0] = (contract(lower1, first) + owner1 * g[...]).reshape(8, 32, W)
    terms[:, 1] = contract(first, lower2).reshape(8, 32, W)
    terms[:, 2] = (contract(lower2, second) + owner2 * g[...]).reshape(8, 32, W)

    for d in range(1, 8):
        qq = (q + d) % 8
        send(terms.at[qq], w1.at[d - 1], p1_s.at[d - 1], p1_r.at[d - 1], dev(x, z, qq))
    total = terms[q]
    for d in range(1, 8):
        arrived(w1.at[d - 1], p1_s.at[d - 1], p1_r.at[d - 1])
        total = total + w1[d - 1]
    for xx in range(4):
        u[xx] = total[:, xx * 8 : (xx + 1) * 8, :]
    for d in range(1, 4):
        send(u.at[xr(d)], w2.at[d - 1], p2_s.at[d - 1], p2_r.at[d - 1], dev(xr(d), z, q))
    total = u[x]
    for d in range(1, 4):
        arrived(w2.at[d - 1], p2_s.at[d - 1], p2_r.at[d - 1])
        total = total + w2[d - 1]
    w3[z] = total
    for d in range(1, 8):
        send(w3.at[z], w3.at[z], p3_s.at[d - 1], p3_r.at[d - 1], dev(x, zr(d), q))
    for d in range(1, 8):
        arrived(w3.at[zr(-d)], p3_s.at[d - 1], p3_r.at[d - 1])
    total = w3[0]
    for zz in range(1, 8):
        total = total + w3[zz]
    w4[x] = total
    for d in range(1, 4):
        send(w4.at[x], w4.at[x], p4_s.at[d - 1], p4_r.at[d - 1], dev(xr(d), z, q))
    for d in range(1, 4):
        arrived(w4.at[xr(-d)], p4_s.at[d - 1], p4_r.at[d - 1])
    for d in range(1, 8):
        send(w4, wf.at[q], p5_s.at[d - 1], p5_r.at[d - 1], dev(x, z, (q + d) % 8))
    wf[q] = w4[...]
    for d in range(1, 8):
        arrived(wf.at[(q - d) % 8], p5_s.at[d - 1], p5_r.at[d - 1])

    first_diag = -wf[:, :, 0].reshape(W, W)
    fd_out[...] = first_diag
    link = -(
        wf[:, :, 1].reshape(W, W)
        + jnp.dot(first_diag.astype(BF16), top[...], preferred_element_type=F32)
    )
    link = link.astype(BF16)
    link_out[...] = link
    sd_out[...] = -wf[:, :, 2].reshape(W, W) - contract(top[...], link)

    for copy in sent:
        copy.wait_send()
    for h in range(2):

        @pl.when(q != z)
        def _(h=h):
            remote(
                lm.at[h, z // 2, z % 2],
                m.at[h, z // 2, x, q, z % 2],
                sc_s.at[h, 0],
                sc_r.at[h, q],
                dev(x, z, z),
            ).wait_send()

        for d in range(1, 8):
            zz = zr(d)
            remote(
                lm.at[h, zz // 2, zz % 2],
                m.at[h, zz // 2, x, q, zz % 2],
                sc_s.at[h, d],
                sc_r.at[h, q],
                dev(x, zz, z),
            ).wait_send()
        for a in range(4):
            remote(
                prod.at[h, a, :, 1 - core],
                r1.at[h, a],
                r1_s.at[h, a],
                r1_r.at[h, a],
                dev(x, z, q + 1 - 2 * core),
            ).wait_send()
            for d in (1, 2, 3):
                y_copy(h, d, a).wait_send()


def per_device(
    anc_inverse,
    first_lower,
    second_lower,
    second_top,
    struct_first,
    struct_keep,
    pivot_h,
    pivot_s,
    shifts,
    pole_index,
):
    vmem = pl.BlockSpec(memory_space=pltpu.VMEM)
    smem = pl.BlockSpec(memory_space=pltpu.SMEM)
    hbm = pl.BlockSpec(memory_space=pl.ANY)
    dma = pltpu.SemaphoreType.DMA
    fc, fd, link, sc, sd = pl.pallas_call(
        body,
        out_shape=(
            jax.ShapeDtypeStruct((4, 32, W), BF16),
            jax.ShapeDtypeStruct((W, W), F32),
            jax.ShapeDtypeStruct((W, W), BF16),
            jax.ShapeDtypeStruct((4, 32, W), BF16),
            jax.ShapeDtypeStruct((W, W), F32),
        ),
        in_specs=[hbm, vmem, vmem, vmem, smem, smem, hbm, hbm, smem, smem],
        out_specs=(vmem,) * 5,
        scratch_shapes=[
            pltpu.VMEM((4, 4096, W), BF16),
            pltpu.VMEM((2, 4096, 128), F32),
            pltpu.VMEM((1024, 4096), BF16),
            pltpu.VMEM((2, 4, 4, 8, 2, 16, W), BF16),
            pltpu.VMEM((2, 4, 2, 16, W), BF16),
            pltpu.VMEM((2, 4, 4, 2, 32, W), F32),
            pltpu.VMEM((2, 4, 4, 32, W), F32),
            pltpu.VMEM((2, 3, 4, 32, W), F32),
            pltpu.VMEM((W, W), F32),
            pltpu.VMEM((W, W), F32),
            pltpu.VMEM((8, 3, 32, W), F32),
            pltpu.VMEM((7, 3, 32, W), F32),
            pltpu.VMEM((4, 3, 8, W), F32),
            pltpu.VMEM((3, 3, 8, W), F32),
            pltpu.VMEM((8, 3, 8, W), F32),
            pltpu.VMEM((4, 3, 8, W), F32),
            pltpu.VMEM((8, 4, 3, 8, W), F32),
            dma((6,)),
            dma((2, 8)),
            dma((2, 8)),
            dma((2,)),
            dma((2, 3)),
            dma((2, 3)),
            dma((2, 4, 2, 2)),
            dma((2, 4, 2, 2)),
            dma((2, 4, 2)),
            dma((2, 4, 2)),
            dma((2, 8, 2)),
            dma((2, 8, 2)),
            dma((2, 8)),
            dma((2, 8)),
            dma((2, 4)),
            dma((2, 4)),
            dma((2, 3, 4)),
            dma((2, 3, 4)),
            dma((7,)),
            dma((7,)),
            dma((3,)),
            dma((3,)),
            dma((7,)),
            dma((7,)),
            dma((3,)),
            dma((3,)),
            dma((7,)),
            dma((7,)),
        ],
        compiler_params=pltpu.CompilerParams(
            collective_id=0, has_side_effects=True, vmem_limit_bytes=56 * 1024 * 1024
        ),
        name="selected_inversion",
    )(
        anc_inverse.reshape(4, 4096, W),
        first_lower.reshape(4, 32, W),
        second_lower.reshape(4, 32, W),
        second_top,
        struct_first,
        struct_keep,
        pivot_h,
        pivot_s,
        shifts,
        pole_index,
    )
    return fc[:, None], fd, link, sc[:, None], sd


def solution(mesh):
    return jax.shard_map(
        per_device,
        mesh=mesh,
        in_specs=(
            P(None, "prow", None, None, "pcol", None),
            P(None, "prow", "pcol", None),
            P(None, "prow", "pcol", None),
            P(),
            P(),
            P(),
            P(),
            P(),
            P(),
            P(),
        ),
        out_specs=(P(None, "prow", "pcol", None), P(), P(), P(None, "prow", "pcol", None), P()),
        check_vma=False,
    )
```

```python
import jax
import jax.numpy as jnp
from jax import lax
from jax.experimental import pallas as pl
from jax.experimental.pallas import tpu as pltpu
from jax.sharding import PartitionSpec as P

MESH = pl.DeviceIdType.MESH
F32 = jnp.float32
BF16 = jnp.bfloat16
HI = lax.Precision.HIGHEST
NX, NZ, NY = 4, 8, 4
W = 256
BLK = 32
LOW = 3


def gauss_jordan(x, first, last):
    n = x.shape[0]
    rows = lax.broadcasted_iota(jnp.int32, (n, n), 0)
    cols = lax.broadcasted_iota(jnp.int32, (n, n), 1)
    row1 = lax.broadcasted_iota(jnp.int32, (n, 1), 0)
    col1 = lax.broadcasted_iota(jnp.int32, (1, n), 1)
    for k in range(first, last):
        inv = 1.0 / x[k : k + 1, k : k + 1]
        right = jnp.where(col1 == k, 1.0, x[k : k + 1, :]) * inv
        left = jnp.where(row1 == k, 1.0, -x[:, k : k + 1])
        x = jnp.where((rows == k) | (cols == k), 0.0, x) + left * right
    return x


def contract(left, right):
    return lax.dot_general(left, right, (((0,), (0,)), ((), ())), preferred_element_type=F32)


def split(value):
    high = value.astype(BF16)
    return high, (value - high.astype(F32)).astype(BF16)


def body(
    anc,
    l1,
    l2,
    top_in,
    keep1_in,
    keep2_in,
    piv_h,
    piv_s,
    shifts_in,
    pole_in,
    fc_out,
    fd_out,
    link_out,
    sc_out,
    sd_out,
    abuf,
    a32,
    abf,
    m,
    ll,
    lm,
    mb,
    mbt,
    prod,
    r1,
    r2,
    g,
    gs,
    gp,
    fc,
    sc,
    fd,
    link,
    sd,
    top,
    keep1,
    keep2,
    shifts,
    pole,
    ta,
    wa0,
    ua,
    wa1,
    wa3,
    wa4,
    waf,
    tb,
    wb0,
    ub,
    wb1,
    wb3,
    wb4,
    wbf,
    load_sem,
    out_sem,
    sc_s,
    sc_r,
    sc_l,
    mb_s,
    mb_r,
    a1_s,
    a1_r,
    a2_s,
    a2_r,
    b1_s,
    b1_r,
    b2_s,
    b2_r,
    b3_s,
    b3_r,
    r1_s,
    r1_r,
    r2_s,
    r2_r,
    p_s,
    p_r,
):
    prow = lax.axis_index("prow")
    q = lax.axis_index("pcol")
    x, z = prow // NZ, prow % NZ
    y, core = q // 2, q % 2

    def dev(xx, zz, qq):
        return {"prow": xx * NZ + zz, "pcol": qq}

    def xr(d):
        return (x + d) % NX

    def zr(d):
        return (z + d) % NZ

    def qr(d):
        return (q + d) % 8

    barrier = pltpu.get_barrier_semaphore()

    def greet(target):
        pl.semaphore_signal(barrier, inc=1, device_id=target, device_id_type=MESH)

    @pl.when(q != z)
    def _():
        for d in range(8):
            greet(dev(x, q, d))

    for d in range(1, 8):
        greet(dev(x, z, qr(d)))
        greet(dev(x, zr(d), q))
    for dx in range(1, 4):
        for dy in range(4):
            greet(dev(xr(dx), z, qr(2 * dy)))

    def load(src, dst, i):
        copy = pltpu.make_async_copy(src, dst, load_sem.at[i])
        copy.start()
        return copy

    factors = [load(l1, ll.at[0], 0), load(l2, ll.at[1], 1)]
    flags = [load(keep1_in, keep1, 2), load(keep2_in, keep2, 3)]
    pivots = [load(piv_h.at[core], g, 4), load(piv_s.at[core], gs, 5)]
    pivots += [load(shifts_in, shifts, 6), load(pole_in, pole, 7)]
    tops = load(top_in, top, 8)
    blocks = [load(anc.at[a], abuf.at[a], 9 + a) for a in range(4)]

    def remote(src, dst, ssem, rsem, target):
        return pltpu.make_async_remote_copy(
            src_ref=src, dst_ref=dst, send_sem=ssem, recv_sem=rsem, device_id=target, device_id_type=MESH
        )

    sent = []

    def send(src, dst, ssem, rsem, target):
        copy = remote(src, dst, ssem, rsem, target)
        copy.start()
        sent.append(copy)

    def arrived(dst, ssem, rsem):
        remote(dst, dst, ssem, rsem, dev(x, z, qr(1))).wait_recv()

    for copy in factors + flags:
        copy.wait()
    flag1 = [keep1[a * (NX * NZ) + prow].astype(F32) for a in range(4)]
    flag2 = [flag1[a] * keep2[a * (NX * NZ) + prow].astype(F32) for a in range(4)]
    for a in range(4):
        lm[0, a] = (ll[0, a].astype(F32) * flag1[a]).astype(BF16)
        lm[1, a] = (ll[1, a].astype(F32) * flag2[a]).astype(BF16)

    pl.semaphore_wait(barrier, 33)

    def slice_of(zz):
        return lm.at[:, zz // 2, pl.ds(pl.multiple_of(16 * (zz % 2), 16), 16)]

    def spread(d):
        zz = zr(d)
        dst = m.at[:, zz // 2, x, q, zz % 2]
        return remote(slice_of(zz), dst, sc_s.at[d], sc_r.at[q], dev(x, zz, z))

    def keep_own():
        return pltpu.make_async_copy(slice_of(z), m.at[:, z // 2, x, q, z % 2], sc_l)

    @pl.when(q == z)
    def _():
        keep_own().start()

    @pl.when(q != z)
    def _():
        spread(0).start()

    for d in range(1, 8):
        spread(d).start()

    def relayout(a):
        blocks[a].wait()

        def widen(i, _):
            rows = pl.ds(pl.multiple_of(i * 512, 512), 512)
            for s in range(2):
                a32[s, rows, :] = abuf[a, rows, s * 128 : (s + 1) * 128].astype(F32)
            return 0

        lax.fori_loop(0, 8, widen, 0)

        def pick(c, _):
            for s in range(2):
                lanes = pl.ds(pl.multiple_of(c * W + s * 128, 128), 128)
                abf[a * W : (a + 1) * W, lanes] = a32[s, pl.ds(c, W, stride=16), :].astype(BF16)
            return 0

        lax.fori_loop(0, 16, pick, 0)

    def inverse_pieces():
        for k in range(W // BLK):
            rows = pl.ds(k * BLK, BLK)
            for part in range(4):
                block = g[rows, k * BLK : (k + 1) * BLK] if part == 0 else gp[...]
                gp[...] = gauss_jordan(block, part * 8, part * 8 + 8)
                yield
            panel = g[rows, :]
            lanes = lax.broadcasted_iota(jnp.int32, (BLK, W), 1)
            unit = (lanes == lax.broadcasted_iota(jnp.int32, (BLK, W), 0) + k * BLK).astype(F32)
            inside = (lanes >= k * BLK) & (lanes < k * BLK + BLK)
            solved = jnp.dot(
                gp[...], jnp.where(inside, -unit, panel), precision=HI, preferred_element_type=F32
            )
            g[...] = g[...] - lax.dot_general(
                panel, solved + unit, (((0,), (0,)), ((), ())), precision=HI, preferred_element_type=F32
            )
            g[rows, :] = solved
            yield

    pieces = inverse_pieces()

    def work(n):
        for _ in range(n):
            next(pieces, None)

    relayout(0)
    for copy in pivots:
        copy.wait()
    g[...] = g[...] + shifts[pole[0]] * gs[...]

    lo, hi = pl.ds(0, LOW), pl.ds(LOW, 8 - LOW)

    def mine(h, zz, part):
        return m.at[h, zz // 2, x, part, zz % 2]

    def group(h, zz, s):
        return m.at[h, zz // 2, pl.ds(2 * s, 2), lo, zz % 2]

    def at_x(h, zz, xx):
        return m.at[h, zz // 2, xx, hi, zz % 2]

    def cross(h, d):
        ref = mine(h, zr(d), hi)
        send(ref, ref, b2_s.at[h, d % 8, 0], b2_r.at[h, d % 8, 0], dev(xr(1), z, q))
        send(ref, ref, b2_s.at[h, d % 8, 1], b2_r.at[h, d % 8, 1], dev(xr(3), z, q))

    def far(i):
        half = (8 - LOW + 1) // 2
        return pl.ds(LOW, half) if i == 0 else pl.ds(LOW + half, 8 - LOW - half)

    def high_first(h):
        ref = mine(h, z, hi)
        for e in (1, -1, 2, -2):
            slot = -e % 8
            send(ref, ref, b1_s.at[h, slot], b1_r.at[h, slot], dev(x, zr(e), q))

    def high_second(h):
        for i, step in enumerate((1, -1)):
            zz = zr(-2 * step)
            slot = -2 * step % 8
            ref = mine(h, zz, hi)
            arrived(ref, b1_s.at[h, slot], b1_r.at[h, slot])
            slot = -3 * step % 8
            send(ref, ref, b1_s.at[h, slot], b1_r.at[h, slot], dev(x, zr(step), q))
            slot = 4 if i == 0 else 0
            ref = mine(h, zz, far(i))
            send(ref, ref, b1_s.at[h, slot], b1_r.at[h, slot], dev(x, zr(2 * step), q))
        for d in (1, -1):
            arrived(mine(h, zr(d), hi), b1_s.at[h, d % 8], b1_r.at[h, d % 8])
        for d in (1, -1, 2, -2):
            cross(h, d)

    def high_third(h):
        for d in (3, -3):
            arrived(mine(h, zr(d), hi), b1_s.at[h, d % 8], b1_r.at[h, d % 8])
            cross(h, d)
        for i, slot in enumerate((4, 0)):
            arrived(mine(h, zr(4), far(i)), b1_s.at[h, slot], b1_r.at[h, slot])
        cross(h, 4)

    def low_z(h, r, s):
        for i, step in enumerate((1, -1)):
            if r == 4 and s != i:
                continue
            ref = group(h, zr(-step * (r - 1)), s)
            send(ref, ref, a2_s.at[h, r - 1, i, s], a2_r.at[h, r - 1, i, s], dev(x, zr(step), q))

    def low_z_wait(h, r, s):
        for i, step in enumerate((1, -1)):
            if r == 4 and s != i:
                continue
            arrived(group(h, zr(-step * r), s), a2_s.at[h, r - 1, i, s], a2_r.at[h, r - 1, i, s])

    def begin():
        @pl.when(q == z)
        def _():
            keep_own().wait()

        @pl.when(q != z)
        def _():
            arrived(m.at[:, z // 2, x, q, z % 2], sc_s.at[0], sc_r.at[q])

        for d in range(1, 8):
            arrived(m.at[:, z // 2, x, qr(d), z % 2], sc_s.at[d], sc_r.at[qr(d)])

    def first_sends(h):
        for d in (1, 3, 2):
            ref = mine(h, z, lo)
            send(ref, ref, a1_s.at[h, d - 1], a1_r.at[h, d - 1], dev(xr(d), z, q))
        high_first(h)
        cross(h, 0)

    def low_start(h):
        for d in (1, 3, 2):
            arrived(m.at[h, z // 2, xr(-d), lo, z % 2], a1_s.at[h, d - 1], a1_r.at[h, d - 1])
        for s in range(2):
            low_z(h, 1, s)

    def low(h, r):
        for s in range(2):
            low_z_wait(h, r, s)
            if r < 4:
                low_z(h, r + 1, s)

    def hop(h, *offsets):
        for d in offsets:
            zz = zr(d)
            slot = d % 8
            arrived(at_x(h, zz, xr(-1)), b2_s.at[h, slot, 0], b2_r.at[h, slot, 0])
            arrived(at_x(h, zz, xr(1)), b2_s.at[h, slot, 1], b2_r.at[h, slot, 1])
            if d in (0, 1, 2, -3):
                ref = at_x(h, zz, xr(-1))
                send(ref, ref, b3_s.at[h, slot], b3_r.at[h, slot], dev(xr(1), z, q))
            else:
                ref = at_x(h, zz, xr(1))
                send(ref, ref, b3_s.at[h, slot], b3_r.at[h, slot], dev(xr(3), z, q))

    def hop_wait(h):
        for d in range(8):
            arrived(at_x(h, zr(d), xr(2)), b3_s.at[h, d], b3_r.at[h, d])

    def pair_copy(h, a):
        return remote(
            prod.at[h, a, :, 1 - core],
            r1.at[h, a],
            r1_s.at[h, a],
            r1_r.at[h, a],
            dev(x, z, q + 1 - 2 * core),
        )

    def y_copy(h, d, a):
        yy = (y + d) % NY
        return remote(
            prod.at[h, a, yy, core],
            r2.at[h, d - 1, a],
            r2_s.at[h, d - 1, a],
            r2_r.at[h, d - 1, a],
            dev(x, z, yy * 2 + core),
        )

    def multiply(h):
        def rows(a, _):
            weights = m[h].reshape(16 * W, W)
            part = jnp.dot(
                abf[pl.ds(pl.multiple_of(a * W, W), W), :], weights, preferred_element_type=F32
            )
            prod[h, a] = part.reshape(4, 2, 32, W)
            pair_copy(h, a).start()
            return 0

        lax.fori_loop(0, 4, rows, 0)

    def pair_sum(h):
        def rows(a, _):
            pair_copy(h, a).wait_recv()
            for yy in range(4):
                prod[h, a, yy, core] = prod[h, a, yy, core] + r1[h, a, yy]
            for d in (2, 1, 3):
                y_copy(h, d, a).start()
            return 0

        lax.fori_loop(0, 4, rows, 0)

    def row_part(h, a):
        total = prod[h, a, y, core]
        for d in (1, 2, 3):
            y_copy(h, d, a).wait_recv()
            total = total + r2[h, d - 1, a]
        return total

    outs = []

    def put(src, dst, i):
        copy = pltpu.make_async_copy(src, dst, out_sem.at[i])
        copy.start()
        outs.append(copy)

    def finish_first():
        for a in range(4):
            fc[a] = (-row_part(0, a) * flag1[a]).astype(BF16)
        put(fc, fc_out, 0)

    def finish_second():
        for a in range(4):
            bridge = jnp.dot(fc[a], top[...], preferred_element_type=F32)
            sc[a] = (-(row_part(1, a) + bridge) * flag2[a]).astype(BF16)
        put(sc, sc_out, 1)

    def share_rows():
        for d in range(1, 8):
            send(lm.at[1], mb.at[:, q], mb_s.at[d - 1], mb_r.at[d - 1], dev(x, z, qr(d)))
        for a in range(4):
            mb[a, q] = lm[1, a]

    def turn_rows():
        for d in range(1, 8):
            arrived(mb.at[:, qr(-d)], mb_s.at[d - 1], mb_r.at[d - 1])
        for a in range(4):
            mbt[a] = mb[a].reshape(W, W).T

    spot = x * NY + y
    others = [(dx, dy) for dx in range(NX) for dy in range(NY) if dx or dy]

    def plane(dx, dy):
        xx, yy = (x + dx) % NX, (y + dy) % NY
        return xx * NY + yy, dev(xx, z, yy * 2 + core)

    def all_reduce(base, t, w0, u, w1, w3, w4, wf):
        def sems(i):
            return p_s.at[base + i], p_r.at[base + i]

        twin = dev(x, z, q + 1 - 2 * core)
        send(t.at[1 - core], w0, *sems(0), twin)
        yield
        arrived(w0, *sems(0))
        u[...] = t[core] + w0[...]
        for i, (dx, dy) in enumerate(others):
            there, target = plane(dx, dy)
            send(u.at[there], w1.at[i], *sems(1 + i), target)
        yield
        total = u[spot]
        for i in range(15):
            arrived(w1.at[i], *sems(1 + i))
            total = total + w1[i]
        w3[z] = total
        for d in range(1, 8):
            send(w3.at[z], w3.at[z], *sems(15 + d), dev(x, zr(d), q))
        yield
        for d in range(1, 8):
            arrived(w3.at[zr(-d)], *sems(15 + d))
        total = w3[0]
        for zz in range(1, 8):
            total = total + w3[zz]
        w4[spot] = total
        for i, (dx, dy) in enumerate(others):
            send(w4.at[spot], w4.at[spot], *sems(23 + i), plane(dx, dy)[1])
        yield
        for i, (dx, dy) in enumerate(others):
            arrived(w4.at[plane(-dx, -dy)[0]], *sems(23 + i))
        send(w4, wf.at[core], *sems(38), twin)
        wf[core] = w4[...]
        yield
        arrived(wf.at[1 - core], *sems(38))
        yield

    reduce_a = all_reduce(0, ta, wa0, ua, wa1, wa3, wa4, waf)
    reduce_b = all_reduce(39, tb, wb0, ub, wb1, wb3, wb4, wbf)

    relayout(1)
    relayout(2)
    begin()
    first_sends(0)
    share_rows()
    relayout(3)
    work(1)
    low_start(0)
    work(1)
    high_second(0)
    work(3)
    low(0, 1)
    high_third(0)
    first_sends(1)
    hop(0, 0, 1, -1, 2, -2)
    work(3)
    low(0, 2)
    low_start(1)
    high_second(1)
    hop(0, 3, -3, 4)
    work(4)
    low(0, 3)
    work(2)
    low(1, 1)
    high_third(1)
    work(2)
    low(0, 4)
    hop_wait(0)
    multiply(0)
    hop(1, 0, 1, -1, 2, -2)
    low(1, 2)
    pair_sum(0)
    hop(1, 3, -3, 4)
    work(6)
    low(1, 3)
    turn_rows()
    work(6)
    low(1, 4)
    hop_wait(1)
    multiply(1)

    owner1 = ((prow == 0) & (q == 0)).astype(F32)
    owner2 = ((prow == 0) & (q == 1)).astype(F32)

    def second_term():
        total = jnp.zeros((W, W), F32)
        for a in range(4):
            for piece in split(prod[1, a].reshape(W, W)):
                total = total + jnp.dot(mbt[a], piece, preferred_element_type=F32)
        return total

    work(40)
    tb[...] = (second_term() - owner2 * g[...]).reshape(2, 16, 1, 8, W)
    next(reduce_b)
    tops.wait()
    finish_first()
    first = fc[...].reshape(128, W)
    ta[:, :, 0] = (contract(lm[0].reshape(128, W), first) + owner1 * g[...]).reshape(2, 16, 8, W)
    ta[:, :, 1] = contract(first, lm[1].reshape(128, W)).reshape(2, 16, 8, W)
    next(reduce_a)
    next(reduce_b)
    next(reduce_a)
    pair_sum(1)
    next(reduce_b)
    next(reduce_a)
    next(reduce_b)
    next(reduce_a)
    finish_second()
    next(reduce_b)
    next(reduce_a)
    next(reduce_a)
    first_diag = -waf[:, :, 0].reshape(W, W)
    fd[...] = first_diag
    put(fd, fd_out, 2)
    cross_sum = waf[:, :, 1].reshape(W, W)
    lower = jnp.dot(first_diag.astype(BF16), top[...], preferred_element_type=F32)
    link[...] = (-(cross_sum + lower)).astype(BF16)
    put(link, link_out, 3)
    tail = -contract(top[...], link[...])
    for piece in split(cross_sum):
        tail = tail + contract(piece, top[...])
    next(reduce_b)
    sd[...] = wbf[:, :, 0].reshape(W, W) + tail
    put(sd, sd_out, 4)

    for copy in sent:
        copy.wait_send()

    @pl.when(q != z)
    def _():
        spread(0).wait_send()

    for d in range(1, 8):
        spread(d).wait_send()
    for h in range(2):
        for a in range(4):
            pair_copy(h, a).wait_send()
            for d in (1, 2, 3):
                y_copy(h, d, a).wait_send()
    for copy in outs:
        copy.wait()


def hand_out(*refs):
    ins, outs, stage, sem = refs[:5], refs[5:10], refs[10:15], refs[15]
    loads = [pltpu.make_async_copy(ins[i], stage[i], sem.at[i]) for i in range(5)]
    stores = [pltpu.make_async_copy(stage[i], outs[i], sem.at[5 + i]) for i in range(5)]
    for copy in loads:
        copy.start()
    for load, store in zip(loads, stores):
        load.wait()
        store.start()
    for copy in stores:
        copy.wait()


def per_device(
    anc_inverse,
    first_lower,
    second_lower,
    second_top,
    struct_first,
    struct_keep,
    pivot_h,
    pivot_s,
    shifts,
    pole_index,
):
    hbm = pl.BlockSpec(memory_space=pl.ANY)
    dma = pltpu.SemaphoreType.DMA
    vmem = pltpu.VMEM
    shapes = (
        jax.ShapeDtypeStruct((4, 32, W), BF16),
        jax.ShapeDtypeStruct((W, W), F32),
        jax.ShapeDtypeStruct((W, W), BF16),
        jax.ShapeDtypeStruct((4, 32, W), BF16),
        jax.ShapeDtypeStruct((W, W), F32),
    )

    def reduce_scratch(count):
        return [
            vmem((2, 16, count, 8, W), F32),
            vmem((16, count, 8, W), F32),
            vmem((16, count, 8, W), F32),
            vmem((15, count, 8, W), F32),
            vmem((8, count, 8, W), F32),
            vmem((16, count, 8, W), F32),
            vmem((2, 16, count, 8, W), F32),
        ]

    results = pl.pallas_call(
        body,
        out_shape=shapes,
        in_specs=[hbm] * 10,
        out_specs=(hbm,) * 5,
        scratch_shapes=[
            vmem((4, 4096, W), BF16),
            vmem((2, 4096, 128), F32),
            vmem((1024, 4096), BF16),
            vmem((2, 4, 4, 8, 2, 16, W), BF16),
            vmem((2, 4, 32, W), BF16),
            vmem((2, 4, 32, W), BF16),
            vmem((4, 8, 32, W), BF16),
            vmem((4, W, W), BF16),
            vmem((2, 4, 4, 2, 32, W), F32),
            vmem((2, 4, 4, 32, W), F32),
            vmem((2, 3, 4, 32, W), F32),
            vmem((W, W), F32),
            vmem((W, W), F32),
            vmem((BLK, BLK), F32),
            vmem((4, 32, W), BF16),
            vmem((4, 32, W), BF16),
            vmem((W, W), F32),
            vmem((W, W), BF16),
            vmem((W, W), F32),
            vmem((W, W), BF16),
            pltpu.SMEM((128,), jnp.int32),
            pltpu.SMEM((128,), jnp.int32),
            pltpu.SMEM((40,), F32),
            pltpu.SMEM((40,), jnp.int32),
        ]
        + reduce_scratch(2)
        + reduce_scratch(1)
        + [
            dma((13,)),
            dma((5,)),
            dma((8,)),
            dma((8,)),
            dma,
            dma((7,)),
            dma((7,)),
            dma((2, 3)),
            dma((2, 3)),
            dma((2, 4, 2, 2)),
            dma((2, 4, 2, 2)),
            dma((2, 8)),
            dma((2, 8)),
            dma((2, 8, 2)),
            dma((2, 8, 2)),
            dma((2, 8)),
            dma((2, 8)),
            dma((2, 4)),
            dma((2, 4)),
            dma((2, 3, 4)),
            dma((2, 3, 4)),
            dma((78,)),
            dma((78,)),
        ],
        compiler_params=pltpu.CompilerParams(
            collective_id=0, has_side_effects=True, vmem_limit_bytes=62 * 1024 * 1024
        ),
        name="selected_inversion",
    )(
        anc_inverse.reshape(4, 4096, W),
        first_lower.reshape(4, 32, W),
        second_lower.reshape(4, 32, W),
        second_top,
        struct_first,
        struct_keep,
        pivot_h,
        pivot_s,
        shifts,
        pole_index,
    )
    fc, fd, link, sc, sd = pl.pallas_call(
        hand_out,
        out_shape=shapes,
        in_specs=[hbm] * 5,
        out_specs=(hbm,) * 5,
        scratch_shapes=[vmem(s.shape, s.dtype) for s in shapes] + [dma((10,))],
        name="outputs",
    )(*results)
    return fc[:, None], fd, link, sc[:, None], sd


def solution(mesh):
    return jax.shard_map(
        per_device,
        mesh=mesh,
        in_specs=(
            P(None, "prow", None, None, "pcol", None),
            P(None, "prow", "pcol", None),
            P(None, "prow", "pcol", None),
            P(),
            P(),
            P(),
            P(),
            P(),
            P(),
            P(),
        ),
        out_specs=(P(None, "prow", "pcol", None), P(), P(), P(None, "prow", "pcol", None), P()),
        check_vma=False,
    )
```

```python
import jax
import jax.numpy as jnp
from jax import lax
from jax.experimental import pallas as pl
from jax.experimental.pallas import tpu as pltpu
from jax.sharding import PartitionSpec as P

MESH = pl.DeviceIdType.MESH
F32 = jnp.float32
BF16 = jnp.bfloat16
HI = lax.Precision.HIGHEST
NX, NZ, NY = 4, 8, 4
W = 256
BLK = 32
LOW = 3
FIRST = 10


def gauss_jordan(x, first, last):
    n, lanes = x.shape
    rows = lax.broadcasted_iota(jnp.int32, (n, lanes), 0)
    cols = lax.broadcasted_iota(jnp.int32, (n, lanes), 1)
    lane = lax.broadcasted_iota(jnp.int32, (1, lanes), 1)
    ahead = [jnp.broadcast_to(x[:, k : k + 1], (n, lanes)) for k in range(first, last)]
    for k in range(first, last):
        col = ahead[k - first]
        inv = 1.0 / col[k : k + 1, :]
        left = jnp.where(rows == k, 1.0, -col)
        for i in range(k + 1, last):
            other = ahead[i - first]
            ahead[i - first] = jnp.where(rows == k, 0.0, other) + left * (other[k : k + 1, :] * inv)
        right = jnp.where(lane == k, 1.0, x[k : k + 1, :]) * inv
        x = jnp.where((rows == k) | (cols == k), 0.0, x) + left * right
    return x


def contract(left, right):
    return lax.dot_general(left, right, (((0,), (0,)), ((), ())), preferred_element_type=F32)


def split(value):
    high = value.astype(BF16)
    return high, (value - high.astype(F32)).astype(BF16)


def body(
    anc,
    l1,
    l2,
    top_in,
    keep1_in,
    keep2_in,
    piv_h,
    piv_s,
    shifts_in,
    pole_in,
    fc_out,
    fd_out,
    link_out,
    sc_out,
    sd_out,
    abuf,
    a32,
    abf,
    m,
    ll,
    lm,
    mb,
    mbt,
    prod,
    r1,
    r2,
    g,
    gs,
    gp,
    dz,
    fc,
    sc,
    fd,
    link,
    sd,
    top,
    keep1,
    keep2,
    shifts,
    pole,
    ta,
    wa0,
    ua,
    wa1,
    wa3,
    wa4,
    waf,
    tb,
    wb0,
    ub,
    wb1,
    wb3,
    wb4,
    wbf,
    load_sem,
    out_sem,
    sc_s,
    sc_r,
    sc_l,
    mb_s,
    mb_r,
    a1_s,
    a1_r,
    a2_s,
    a2_r,
    b1_s,
    b1_r,
    b2_s,
    b2_r,
    b3_s,
    b3_r,
    r1_s,
    r1_r,
    r2_s,
    r2_r,
    p_s,
    p_r,
):
    prow = lax.axis_index("prow")
    q = lax.axis_index("pcol")
    x, z = prow // NZ, prow % NZ
    y, core = q // 2, q % 2

    def dev(xx, zz, qq):
        return {"prow": xx * NZ + zz, "pcol": qq}

    def xr(d):
        return (x + d) % NX

    def zr(d):
        return (z + d) % NZ

    def qr(d):
        return (q + d) % 8

    barrier = pltpu.get_barrier_semaphore()

    def greet(target):
        pl.semaphore_signal(barrier, inc=1, device_id=target, device_id_type=MESH)

    @pl.when(q != z)
    def _():
        for d in range(8):
            greet(dev(x, q, d))

    for d in range(1, 8):
        greet(dev(x, z, qr(d)))
        greet(dev(x, zr(d), q))
    for dx in range(1, 4):
        for dy in range(4):
            greet(dev(xr(dx), z, qr(2 * dy)))

    def load(src, dst, i):
        copy = pltpu.make_async_copy(src, dst, load_sem.at[i])
        copy.start()
        return copy

    factors = [load(l1, ll.at[0], 0), load(l2, ll.at[1], 1)]
    flags = [load(keep1_in, keep1, 2), load(keep2_in, keep2, 3)]
    pivots = [load(piv_h.at[core], g, 4), load(piv_s.at[core], gs, 5)]
    pivots += [load(shifts_in, shifts, 6), load(pole_in, pole, 7)]
    tops = load(top_in, top, 8)
    blocks = [load(anc.at[a], abuf.at[a], 9 + a) for a in range(4)]

    def remote(src, dst, ssem, rsem, target):
        return pltpu.make_async_remote_copy(
            src_ref=src, dst_ref=dst, send_sem=ssem, recv_sem=rsem, device_id=target, device_id_type=MESH
        )

    sent = []

    def send(src, dst, ssem, rsem, target):
        copy = remote(src, dst, ssem, rsem, target)
        copy.start()
        sent.append(copy)

    def arrived(dst, ssem, rsem):
        remote(dst, dst, ssem, rsem, dev(x, z, qr(1))).wait_recv()

    for copy in factors + flags:
        copy.wait()
    flag1 = [keep1[a * (NX * NZ) + prow].astype(F32) for a in range(4)]
    flag2 = [flag1[a] * keep2[a * (NX * NZ) + prow].astype(F32) for a in range(4)]
    for a in range(4):
        lm[0, a] = (ll[0, a].astype(F32) * flag1[a]).astype(BF16)
        lm[1, a] = (ll[1, a].astype(F32) * flag2[a]).astype(BF16)

    def inverse_pieces():
        for k in range(W // BLK):
            rows = pl.ds(k * BLK, BLK)
            for part in range(4):
                if part == 0:
                    start = k * BLK // 128 * 128
                    block = g[rows, start : start + 128]
                    if k * BLK > start:
                        block = pltpu.roll(block, 128 - (k * BLK - start), axis=1)
                else:
                    block = gp[...]
                gp[...] = gauss_jordan(block, part * 8, part * 8 + 8)
                yield
            panel = g[rows, :]
            lanes = lax.broadcasted_iota(jnp.int32, (BLK, W), 1)
            unit = (lanes == lax.broadcasted_iota(jnp.int32, (BLK, W), 0) + k * BLK).astype(F32)
            inside = (lanes >= k * BLK) & (lanes < k * BLK + BLK)
            solved = jnp.dot(
                gp[:, :BLK], jnp.where(inside, -unit, panel), precision=HI, preferred_element_type=F32
            )
            g[...] = g[...] - lax.dot_general(
                panel, solved + unit, (((0,), (0,)), ((), ())), precision=HI, preferred_element_type=F32
            )
            g[rows, :] = solved
            yield

    pieces = inverse_pieces()

    def work(n):
        for _ in range(n):
            next(pieces, None)

    for copy in pivots:
        copy.wait()
    g[...] = g[...] + shifts[pole[0]] * gs[...]
    work(FIRST)
    pl.semaphore_wait(barrier, 33)

    def slice_of(h, zz):
        return lm.at[h, zz // 2, pl.ds(pl.multiple_of(16 * (zz % 2), 16), 16)]

    def spread(h, d):
        zz = zr(d)
        dst = m.at[h, zz // 2, x, q, zz % 2]
        return remote(slice_of(h, zz), dst, sc_s.at[h, d], sc_r.at[h, q], dev(x, zz, z))

    def keep_own(h):
        return pltpu.make_async_copy(slice_of(h, z), m.at[h, z // 2, x, q, z % 2], sc_l.at[h])

    def scatter(h):
        @pl.when(q == z)
        def _():
            keep_own(h).start()

        @pl.when(q != z)
        def _():
            spread(h, 0).start()

        for d in range(1, 8):
            spread(h, d).start()

    scatter(0)
    scatter(1)

    def relayout(a):
        blocks[a].wait()

        def widen(i, _):
            rows = pl.ds(pl.multiple_of(i * 512, 512), 512)
            for s in range(2):
                a32[s, rows, :] = abuf[a, rows, s * 128 : (s + 1) * 128].astype(F32)
            return 0

        lax.fori_loop(0, 8, widen, 0)

        def pick(c, _):
            for s in range(2):
                lanes = pl.ds(pl.multiple_of(c * W + s * 128, 128), 128)
                abf[a * W : (a + 1) * W, lanes] = a32[s, pl.ds(c, W, stride=16), :].astype(BF16)
            return 0

        lax.fori_loop(0, 16, pick, 0)

    lo, hi = pl.ds(0, LOW), pl.ds(LOW, 8 - LOW)

    def mine(h, zz, part):
        return m.at[h, zz // 2, x, part, zz % 2]

    def group(h, zz, s):
        return m.at[h, zz // 2, pl.ds(2 * s, 2), lo, zz % 2]

    def at_x(h, zz, xx):
        return m.at[h, zz // 2, xx, hi, zz % 2]

    def cross(h, d):
        ref = mine(h, zr(d), hi)
        send(ref, ref, b2_s.at[h, d % 8, 0], b2_r.at[h, d % 8, 0], dev(xr(1), z, q))
        send(ref, ref, b2_s.at[h, d % 8, 1], b2_r.at[h, d % 8, 1], dev(xr(3), z, q))

    def far(i):
        half = (8 - LOW + 1) // 2
        return pl.ds(LOW, half) if i == 0 else pl.ds(LOW + half, 8 - LOW - half)

    def high_first(h):
        ref = mine(h, z, hi)
        for e in (1, -1, 2, -2):
            slot = -e % 8
            send(ref, ref, b1_s.at[h, slot], b1_r.at[h, slot], dev(x, zr(e), q))

    def high_second(h):
        for i, step in enumerate((1, -1)):
            zz = zr(-2 * step)
            slot = -2 * step % 8
            ref = mine(h, zz, hi)
            arrived(ref, b1_s.at[h, slot], b1_r.at[h, slot])
            slot = -3 * step % 8
            send(ref, ref, b1_s.at[h, slot], b1_r.at[h, slot], dev(x, zr(step), q))
            slot = 4 if i == 0 else 0
            ref = mine(h, zz, far(i))
            send(ref, ref, b1_s.at[h, slot], b1_r.at[h, slot], dev(x, zr(2 * step), q))
        for d in (1, -1):
            arrived(mine(h, zr(d), hi), b1_s.at[h, d % 8], b1_r.at[h, d % 8])
        for d in (1, -1, 2, -2):
            cross(h, d)

    def high_third(h):
        for d in (3, -3):
            arrived(mine(h, zr(d), hi), b1_s.at[h, d % 8], b1_r.at[h, d % 8])
            cross(h, d)
        for i, slot in enumerate((4, 0)):
            arrived(mine(h, zr(4), far(i)), b1_s.at[h, slot], b1_r.at[h, slot])
        cross(h, 4)

    def low_z(h, r, s):
        for i, step in enumerate((1, -1)):
            if r == 4 and s != i:
                continue
            ref = group(h, zr(-step * (r - 1)), s)
            send(ref, ref, a2_s.at[h, r - 1, i, s], a2_r.at[h, r - 1, i, s], dev(x, zr(step), q))

    def low_z_wait(h, r, s):
        for i, step in enumerate((1, -1)):
            if r == 4 and s != i:
                continue
            arrived(group(h, zr(-step * r), s), a2_s.at[h, r - 1, i, s], a2_r.at[h, r - 1, i, s])

    def begin(h):
        @pl.when(q == z)
        def _():
            keep_own(h).wait()

        @pl.when(q != z)
        def _():
            arrived(m.at[h, z // 2, x, q, z % 2], sc_s.at[h, 0], sc_r.at[h, q])

        for d in range(1, 8):
            arrived(m.at[h, z // 2, x, qr(d), z % 2], sc_s.at[h, d], sc_r.at[h, qr(d)])

    def first_sends(h):
        for d in (1, 3, 2):
            ref = mine(h, z, lo)
            send(ref, ref, a1_s.at[h, d - 1], a1_r.at[h, d - 1], dev(xr(d), z, q))
        high_first(h)
        cross(h, 0)

    def low_start(h):
        for d in (1, 3, 2):
            arrived(m.at[h, z // 2, xr(-d), lo, z % 2], a1_s.at[h, d - 1], a1_r.at[h, d - 1])
        for s in range(2):
            low_z(h, 1, s)
            if h == 0:
                jump(h, 0, 2, s)

    def jump(h, origin, r, s):
        for i, step in enumerate((1, -1)):
            if r == 4 and s != i:
                continue
            ref = group(h, zr(-step * origin), s)
            target = dev(x, zr(step * (r - origin)), q)
            send(ref, ref, a2_s.at[h, r - 1, i, s], a2_r.at[h, r - 1, i, s], target)

    def low_far(h):
        for s in range(2):
            low_z_wait(h, 2, s)
            jump(h, 2, 3, s)
            jump(h, 2, 4, s)

    def low_rest(h):
        for r in (1, 3, 4):
            for s in range(2):
                low_z_wait(h, r, s)

    def low(h, r):
        for s in range(2):
            low_z_wait(h, r, s)
            if r < 4:
                low_z(h, r + 1, s)

    def hop(h, *offsets):
        for d in offsets:
            zz = zr(d)
            slot = d % 8
            arrived(at_x(h, zz, xr(-1)), b2_s.at[h, slot, 0], b2_r.at[h, slot, 0])
            arrived(at_x(h, zz, xr(1)), b2_s.at[h, slot, 1], b2_r.at[h, slot, 1])
            if d in (0, 1, 2, -3):
                ref = at_x(h, zz, xr(-1))
                send(ref, ref, b3_s.at[h, slot], b3_r.at[h, slot], dev(xr(1), z, q))
            else:
                ref = at_x(h, zz, xr(1))
                send(ref, ref, b3_s.at[h, slot], b3_r.at[h, slot], dev(xr(3), z, q))

    def hop_wait(h):
        for d in range(8):
            arrived(at_x(h, zr(d), xr(2)), b3_s.at[h, d], b3_r.at[h, d])

    def pair_copy(h, a):
        return remote(
            prod.at[h, a, :, 1 - core],
            r1.at[h, a],
            r1_s.at[h, a],
            r1_r.at[h, a],
            dev(x, z, q + 1 - 2 * core),
        )

    def y_copy(h, d, a):
        yy = (y + d) % NY
        return remote(
            prod.at[h, a, yy, core],
            r2.at[h, d - 1, a],
            r2_s.at[h, d - 1, a],
            r2_r.at[h, d - 1, a],
            dev(x, z, yy * 2 + core),
        )

    def multiply(h):
        def rows(a, _):
            weights = m[h].reshape(16 * W, W)
            part = jnp.dot(
                abf[pl.ds(pl.multiple_of(a * W, W), W), :], weights, preferred_element_type=F32
            )
            prod[h, a] = part.reshape(4, 2, 32, W)
            pair_copy(h, a).start()
            return 0

        lax.fori_loop(0, 4, rows, 0)

    def pair_sum(h):
        def rows(a, _):
            pair_copy(h, a).wait_recv()
            for yy in range(4):
                prod[h, a, yy, core] = prod[h, a, yy, core] + r1[h, a, yy]
            for d in (2, 1, 3):
                y_copy(h, d, a).start()
            return 0

        lax.fori_loop(0, 4, rows, 0)

    def row_part(h, a):
        total = prod[h, a, y, core]
        for d in (1, 2, 3):
            y_copy(h, d, a).wait_recv()
            total = total + r2[h, d - 1, a]
        return total

    outs = []

    def put(src, dst, i):
        copy = pltpu.make_async_copy(src, dst, out_sem.at[i])
        copy.start()
        outs.append(copy)

    def finish_first():
        for a in range(4):
            fc[a] = (-row_part(0, a) * flag1[a]).astype(BF16)
        put(fc, fc_out, 0)

    def finish_second():
        for a in range(4):
            bridge = jnp.dot(fc[a], top[...], preferred_element_type=F32)
            sc[a] = (-(row_part(1, a) + bridge) * flag2[a]).astype(BF16)
        put(sc, sc_out, 1)

    def share_rows():
        for d in range(1, 8):
            send(lm.at[1], mb.at[:, q], mb_s.at[d - 1], mb_r.at[d - 1], dev(x, z, qr(d)))
        for a in range(4):
            mb[a, q] = lm[1, a]

    def turn_rows():
        for d in range(1, 8):
            arrived(mb.at[:, qr(-d)], mb_s.at[d - 1], mb_r.at[d - 1])
        for a in range(4):
            mbt[a] = mb[a].reshape(W, W).T

    spot = x * NY + y
    others = [(dx, dy) for dx in range(NX) for dy in range(NY) if dx or dy]

    def plane(dx, dy):
        xx, yy = (x + dx) % NX, (y + dy) % NY
        return xx * NY + yy, dev(xx, z, yy * 2 + core)

    half = pl.ds(pl.multiple_of((1 - core) * 128, 128), 128)

    def swap_inverse():
        send(g.at[half], dz, p_s.at[78], p_r.at[78], dev(x, z, q + 1 - 2 * core))

    def inverse_rows(k):
        own = g[pl.ds(pl.multiple_of((core * 16 + spot) * 8, 8), 8), :]
        other = dz[pl.ds(pl.multiple_of(spot * 8, 8), 8), :]
        return jnp.where(z == 0, jnp.where(core == k, own, other), 0.0)

    def all_reduce(base, t, w0, u, w1, w3, w4, wf, enter):
        def sems(i):
            return p_s.at[base + i], p_r.at[base + i]

        twin = dev(x, z, q + 1 - 2 * core)
        send(t.at[1 - core], w0, *sems(0), twin)
        yield
        arrived(w0, *sems(0))
        u[...] = t[core] + w0[...]
        for i, (dx, dy) in enumerate(others):
            there, target = plane(dx, dy)
            send(u.at[there], w1.at[i], *sems(1 + i), target)
        yield
        total = u[spot]
        for i in range(15):
            arrived(w1.at[i], *sems(1 + i))
            total = total + w1[i]
        enter(w3, total)
        for d in range(1, 8):
            send(w3.at[z], w3.at[z], *sems(15 + d), dev(x, zr(d), q))
        yield
        for d in range(1, 8):
            arrived(w3.at[zr(-d)], *sems(15 + d))
        total = w3[0]
        for zz in range(1, 8):
            total = total + w3[zz]
        w4[spot] = total
        for i, (dx, dy) in enumerate(others):
            send(w4.at[spot], w4.at[spot], *sems(23 + i), plane(dx, dy)[1])
        yield
        for i, (dx, dy) in enumerate(others):
            arrived(w4.at[plane(-dx, -dy)[0]], *sems(23 + i))
        send(w4, wf.at[core], *sems(38), twin)
        wf[core] = w4[...]
        yield
        arrived(wf.at[1 - core], *sems(38))
        yield

    def enter_a(w3, total):
        w3[z, 0] = total[0] + inverse_rows(0)
        w3[z, 1] = total[1]

    def enter_b(w3, total):
        w3[z, 0] = total[0] - inverse_rows(1)

    reduce_a = all_reduce(0, ta, wa0, ua, wa1, wa3, wa4, waf, enter_a)
    reduce_b = all_reduce(39, tb, wb0, ub, wb1, wb3, wb4, wbf, enter_b)

    relayout(0)
    relayout(1)
    work(5)
    begin(0)
    first_sends(0)
    share_rows()
    relayout(2)
    begin(1)
    work(2)
    low_start(0)
    high_second(0)
    work(4)
    first_sends(1)
    relayout(3)
    work(3)
    low_far(0)
    high_third(0)
    hop(0, 0, 1, -1, 2, -2)
    low_start(1)
    high_second(1)
    work(4)
    hop(0, 3, -3, 4)
    low_rest(0)
    hop_wait(0)
    multiply(0)
    low(1, 1)
    high_third(1)
    pair_sum(0)
    hop(1, 0, 1, -1, 2, -2)
    work(8)
    low(1, 2)
    hop(1, 3, -3, 4)
    work(8)
    turn_rows()
    low(1, 3)
    work(8)
    tops.wait()
    finish_first()
    first = fc[...].reshape(128, W)
    ta[:, :, 0] = contract(lm[0].reshape(128, W), first).reshape(2, 16, 8, W)
    ta[:, :, 1] = contract(first, lm[1].reshape(128, W)).reshape(2, 16, 8, W)
    next(reduce_a)
    low(1, 4)
    next(reduce_a)
    hop_wait(1)
    multiply(1)

    def second_term():
        total = jnp.zeros((W, W), F32)
        for a in range(4):
            for piece in split(prod[1, a].reshape(W, W)):
                total = total + jnp.dot(mbt[a], piece, preferred_element_type=F32)
        return total

    tb[...] = second_term().reshape(2, 16, 1, 8, W)
    next(reduce_b)
    work(1)
    next(reduce_b)
    work(40)
    swap_inverse()
    pair_sum(1)
    arrived(dz, p_s.at[78], p_r.at[78])
    next(reduce_a)
    next(reduce_b)
    next(reduce_a)
    next(reduce_b)
    next(reduce_a)
    finish_second()
    next(reduce_a)
    first_diag = -waf[:, :, 0].reshape(W, W)
    fd[...] = first_diag
    put(fd, fd_out, 2)
    cross_sum = waf[:, :, 1].reshape(W, W)
    lower = jnp.dot(first_diag.astype(BF16), top[...], preferred_element_type=F32)
    link[...] = (-(cross_sum + lower)).astype(BF16)
    put(link, link_out, 3)
    tail = -contract(top[...], link[...])
    for piece in split(cross_sum):
        tail = tail + contract(piece, top[...])
    next(reduce_b)
    next(reduce_b)
    sd[...] = wbf[:, :, 0].reshape(W, W) + tail
    put(sd, sd_out, 4)

    for copy in sent:
        copy.wait_send()

    for h in range(2):

        @pl.when(q != z)
        def _(h=h):
            spread(h, 0).wait_send()

        for d in range(1, 8):
            spread(h, d).wait_send()
        for a in range(4):
            pair_copy(h, a).wait_send()
            for d in (1, 2, 3):
                y_copy(h, d, a).wait_send()
    for copy in outs:
        copy.wait()


def hand_out(*refs):
    ins, outs, stage, sem = refs[:5], refs[5:10], refs[10:15], refs[15]
    loads = [pltpu.make_async_copy(ins[i], stage[i], sem.at[i]) for i in range(5)]
    stores = [pltpu.make_async_copy(stage[i], outs[i], sem.at[5 + i]) for i in range(5)]
    for copy in loads:
        copy.start()
    for load, store in zip(loads, stores):
        load.wait()
        store.start()
    for copy in stores:
        copy.wait()


def per_device(
    anc_inverse,
    first_lower,
    second_lower,
    second_top,
    struct_first,
    struct_keep,
    pivot_h,
    pivot_s,
    shifts,
    pole_index,
):
    hbm = pl.BlockSpec(memory_space=pl.ANY)
    dma = pltpu.SemaphoreType.DMA
    vmem = pltpu.VMEM
    shapes = (
        jax.ShapeDtypeStruct((4, 32, W), BF16),
        jax.ShapeDtypeStruct((W, W), F32),
        jax.ShapeDtypeStruct((W, W), BF16),
        jax.ShapeDtypeStruct((4, 32, W), BF16),
        jax.ShapeDtypeStruct((W, W), F32),
    )

    def reduce_scratch(count):
        return [
            vmem((2, 16, count, 8, W), F32),
            vmem((16, count, 8, W), F32),
            vmem((16, count, 8, W), F32),
            vmem((15, count, 8, W), F32),
            vmem((8, count, 8, W), F32),
            vmem((16, count, 8, W), F32),
            vmem((2, 16, count, 8, W), F32),
        ]

    results = pl.pallas_call(
        body,
        out_shape=shapes,
        in_specs=[hbm] * 10,
        out_specs=(hbm,) * 5,
        scratch_shapes=[
            vmem((4, 4096, W), BF16),
            vmem((2, 4096, 128), F32),
            vmem((1024, 4096), BF16),
            vmem((2, 4, 4, 8, 2, 16, W), BF16),
            vmem((2, 4, 32, W), BF16),
            vmem((2, 4, 32, W), BF16),
            vmem((4, 8, 32, W), BF16),
            vmem((4, W, W), BF16),
            vmem((2, 4, 4, 2, 32, W), F32),
            vmem((2, 4, 4, 32, W), F32),
            vmem((2, 3, 4, 32, W), F32),
            vmem((W, W), F32),
            vmem((W, W), F32),
            vmem((BLK, 128), F32),
            vmem((128, W), F32),
            vmem((4, 32, W), BF16),
            vmem((4, 32, W), BF16),
            vmem((W, W), F32),
            vmem((W, W), BF16),
            vmem((W, W), F32),
            vmem((W, W), BF16),
            pltpu.SMEM((128,), jnp.int32),
            pltpu.SMEM((128,), jnp.int32),
            pltpu.SMEM((40,), F32),
            pltpu.SMEM((40,), jnp.int32),
        ]
        + reduce_scratch(2)
        + reduce_scratch(1)
        + [
            dma((13,)),
            dma((5,)),
            dma((2, 8)),
            dma((2, 8)),
            dma((2,)),
            dma((7,)),
            dma((7,)),
            dma((2, 3)),
            dma((2, 3)),
            dma((2, 4, 2, 2)),
            dma((2, 4, 2, 2)),
            dma((2, 8)),
            dma((2, 8)),
            dma((2, 8, 2)),
            dma((2, 8, 2)),
            dma((2, 8)),
            dma((2, 8)),
            dma((2, 4)),
            dma((2, 4)),
            dma((2, 3, 4)),
            dma((2, 3, 4)),
            dma((79,)),
            dma((79,)),
        ],
        compiler_params=pltpu.CompilerParams(
            collective_id=0, has_side_effects=True, vmem_limit_bytes=62 * 1024 * 1024
        ),
        name="selected_inversion",
    )(
        anc_inverse.reshape(4, 4096, W),
        first_lower.reshape(4, 32, W),
        second_lower.reshape(4, 32, W),
        second_top,
        struct_first,
        struct_keep,
        pivot_h,
        pivot_s,
        shifts,
        pole_index,
    )
    fc, fd, link, sc, sd = pl.pallas_call(
        hand_out,
        out_shape=shapes,
        in_specs=[hbm] * 5,
        out_specs=(hbm,) * 5,
        scratch_shapes=[vmem(s.shape, s.dtype) for s in shapes] + [dma((10,))],
        name="outputs",
    )(*results)
    return fc[:, None], fd, link, sc[:, None], sd


def solution(mesh):
    return jax.shard_map(
        per_device,
        mesh=mesh,
        in_specs=(
            P(None, "prow", None, None, "pcol", None),
            P(None, "prow", "pcol", None),
            P(None, "prow", "pcol", None),
            P(),
            P(),
            P(),
            P(),
            P(),
            P(),
            P(),
        ),
        out_specs=(P(None, "prow", "pcol", None), P(), P(), P(None, "prow", "pcol", None), P()),
        check_vma=False,
    )
```

```python
import jax
import jax.numpy as jnp
from jax import lax
from jax.experimental import pallas as pl
from jax.experimental.pallas import tpu as pltpu
from jax.sharding import PartitionSpec as P

MESH = pl.DeviceIdType.MESH
F32 = jnp.float32
BF16 = jnp.bfloat16
HI = lax.Precision.HIGHEST
NX, NZ, NY = 4, 8, 4
W = 256
BLK = 32
LOW = 3
FIRST = 10


def gauss_jordan(x, first, last):
    n, lanes = x.shape
    rows = lax.broadcasted_iota(jnp.int32, (n, lanes), 0)
    cols = lax.broadcasted_iota(jnp.int32, (n, lanes), 1)
    lane = lax.broadcasted_iota(jnp.int32, (1, lanes), 1)
    ahead = [jnp.broadcast_to(x[:, k : k + 1], (n, lanes)) for k in range(first, last)]
    for k in range(first, last):
        col = ahead[k - first]
        inv = 1.0 / col[k : k + 1, :]
        left = jnp.where(rows == k, 1.0, -col)
        for i in range(k + 1, last):
            other = ahead[i - first]
            ahead[i - first] = jnp.where(rows == k, 0.0, other) + left * (other[k : k + 1, :] * inv)
        right = jnp.where(lane == k, 1.0, x[k : k + 1, :]) * inv
        x = jnp.where((rows == k) | (cols == k), 0.0, x) + left * right
    return x


def contract(left, right):
    return lax.dot_general(left, right, (((0,), (0,)), ((), ())), preferred_element_type=F32)


def split(value):
    high = value.astype(BF16)
    return high, (value - high.astype(F32)).astype(BF16)


def body(
    anc,
    l1,
    l2,
    top_in,
    keep1_in,
    keep2_in,
    piv_h,
    piv_s,
    shifts_in,
    pole_in,
    fc_out,
    fd_out,
    link_out,
    sc_out,
    sd_out,
    abuf,
    a32,
    abf,
    m,
    ll,
    lm,
    mb,
    mbt,
    prod,
    r1,
    r2,
    g,
    gs,
    gp,
    dz,
    fc,
    sc,
    fd,
    link,
    sd,
    top,
    keep1,
    keep2,
    shifts,
    pole,
    ta,
    wa0,
    ua,
    wa1,
    wa3,
    wa4,
    waf,
    tb,
    wb0,
    ub,
    wb1,
    wb3,
    wb4,
    wbf,
    load_sem,
    out_sem,
    sc_s,
    sc_r,
    sc_l,
    mb_s,
    mb_r,
    a1_s,
    a1_r,
    a2_s,
    a2_r,
    b1_s,
    b1_r,
    b2_s,
    b2_r,
    b3_s,
    b3_r,
    r1_s,
    r1_r,
    r2_s,
    r2_r,
    p_s,
    p_r,
):
    prow = lax.axis_index("prow")
    q = lax.axis_index("pcol")
    x, z = prow // NZ, prow % NZ
    y, core = q // 2, q % 2

    def dev(xx, zz, qq):
        return {"prow": xx * NZ + zz, "pcol": qq}

    def xr(d):
        return (x + d) % NX

    def zr(d):
        return (z + d) % NZ

    def qr(d):
        return (q + d) % 8

    barrier = pltpu.get_barrier_semaphore()

    def greet(target):
        pl.semaphore_signal(barrier, inc=1, device_id=target, device_id_type=MESH)

    @pl.when(q != z)
    def _():
        for d in range(8):
            greet(dev(x, q, d))

    for d in range(1, 8):
        greet(dev(x, z, qr(d)))
        greet(dev(x, zr(d), q))
    for dx in range(1, 4):
        for dy in range(4):
            greet(dev(xr(dx), z, qr(2 * dy)))

    def load(src, dst, i):
        copy = pltpu.make_async_copy(src, dst, load_sem.at[i])
        copy.start()
        return copy

    factors = [load(l1, ll.at[0], 0), load(l2, ll.at[1], 1)]
    flags = [load(keep1_in, keep1, 2), load(keep2_in, keep2, 3)]
    pivots = [load(piv_h.at[core], g, 4), load(piv_s.at[core], gs, 5)]
    pivots += [load(shifts_in, shifts, 6), load(pole_in, pole, 7)]
    tops = load(top_in, top, 8)
    blocks = [load(anc.at[a], abuf.at[a], 9 + a) for a in range(4)]

    def remote(src, dst, ssem, rsem, target):
        return pltpu.make_async_remote_copy(
            src_ref=src, dst_ref=dst, send_sem=ssem, recv_sem=rsem, device_id=target, device_id_type=MESH
        )

    sent = []

    def send(src, dst, ssem, rsem, target):
        copy = remote(src, dst, ssem, rsem, target)
        copy.start()
        sent.append(copy)

    def arrived(dst, ssem, rsem):
        remote(dst, dst, ssem, rsem, dev(x, z, qr(1))).wait_recv()

    for copy in factors + flags:
        copy.wait()
    flag1 = [keep1[a * (NX * NZ) + prow].astype(F32) for a in range(4)]
    flag2 = [flag1[a] * keep2[a * (NX * NZ) + prow].astype(F32) for a in range(4)]
    for a in range(4):
        lm[0, a] = (ll[0, a].astype(F32) * flag1[a]).astype(BF16)
        lm[1, a] = (ll[1, a].astype(F32) * flag2[a]).astype(BF16)

    def inverse_pieces():
        for k in range(W // BLK):
            rows = pl.ds(k * BLK, BLK)
            for part in range(4):
                if part == 0:
                    start = k * BLK // 128 * 128
                    block = g[rows, start : start + 128]
                    if k * BLK > start:
                        block = pltpu.roll(block, 128 - (k * BLK - start), axis=1)
                else:
                    block = gp[...]
                gp[...] = gauss_jordan(block, part * 8, part * 8 + 8)
                yield
            panel = g[rows, :]
            lanes = lax.broadcasted_iota(jnp.int32, (BLK, W), 1)
            unit = (lanes == lax.broadcasted_iota(jnp.int32, (BLK, W), 0) + k * BLK).astype(F32)
            inside = (lanes >= k * BLK) & (lanes < k * BLK + BLK)
            solved = jnp.dot(
                gp[:, :BLK], jnp.where(inside, -unit, panel), precision=HI, preferred_element_type=F32
            )
            g[...] = g[...] - lax.dot_general(
                panel, solved + unit, (((0,), (0,)), ((), ())), precision=HI, preferred_element_type=F32
            )
            g[rows, :] = solved
            yield

    pieces = inverse_pieces()

    def work(n):
        for _ in range(n):
            next(pieces, None)

    for copy in pivots:
        copy.wait()
    g[...] = g[...] + shifts[pole[0]] * gs[...]
    work(FIRST)
    pl.semaphore_wait(barrier, 33)

    def slice_of(h, zz):
        return lm.at[h, zz // 2, pl.ds(pl.multiple_of(16 * (zz % 2), 16), 16)]

    def spread(h, d):
        zz = zr(d)
        dst = m.at[h, zz // 2, x, q, zz % 2]
        return remote(slice_of(h, zz), dst, sc_s.at[h, d], sc_r.at[h, q], dev(x, zz, z))

    def keep_own(h):
        return pltpu.make_async_copy(slice_of(h, z), m.at[h, z // 2, x, q, z % 2], sc_l.at[h])

    def scatter(h):
        @pl.when(q == z)
        def _():
            keep_own(h).start()

        @pl.when(q != z)
        def _():
            spread(h, 0).start()

        for d in range(1, 8):
            spread(h, d).start()

    scatter(0)
    scatter(1)

    def relayout(a):
        blocks[a].wait()

        def widen(i, _):
            rows = pl.ds(pl.multiple_of(i * 512, 512), 512)
            for s in range(2):
                a32[s, rows, :] = abuf[a, rows, s * 128 : (s + 1) * 128].astype(F32)
            return 0

        lax.fori_loop(0, 8, widen, 0)

        def pick(c, _):
            for s in range(2):
                lanes = pl.ds(pl.multiple_of(c * W + s * 128, 128), 128)
                abf[a * W : (a + 1) * W, lanes] = a32[s, pl.ds(c, W, stride=16), :].astype(BF16)
            return 0

        lax.fori_loop(0, 16, pick, 0)

    lo, hi = pl.ds(0, LOW), pl.ds(LOW, 8 - LOW)

    def mine(h, zz, part):
        return m.at[h, zz // 2, x, part, zz % 2]

    def group(h, zz, s):
        return m.at[h, zz // 2, pl.ds(2 * s, 2), lo, zz % 2]

    def at_x(h, zz, xx):
        return m.at[h, zz // 2, xx, hi, zz % 2]

    def cross(h, d):
        ref = mine(h, zr(d), hi)
        send(ref, ref, b2_s.at[h, d % 8, 0], b2_r.at[h, d % 8, 0], dev(xr(1), z, q))
        send(ref, ref, b2_s.at[h, d % 8, 1], b2_r.at[h, d % 8, 1], dev(xr(3), z, q))

    def far(i):
        half = (8 - LOW + 1) // 2
        return pl.ds(LOW, half) if i == 0 else pl.ds(LOW + half, 8 - LOW - half)

    def high_first(h):
        ref = mine(h, z, hi)
        for e in (1, -1, 2, -2):
            slot = -e % 8
            send(ref, ref, b1_s.at[h, slot], b1_r.at[h, slot], dev(x, zr(e), q))

    def high_second(h):
        for i, step in enumerate((1, -1)):
            zz = zr(-2 * step)
            slot = -2 * step % 8
            ref = mine(h, zz, hi)
            arrived(ref, b1_s.at[h, slot], b1_r.at[h, slot])
            slot = -3 * step % 8
            send(ref, ref, b1_s.at[h, slot], b1_r.at[h, slot], dev(x, zr(step), q))
            slot = 4 if i == 0 else 0
            ref = mine(h, zz, far(i))
            send(ref, ref, b1_s.at[h, slot], b1_r.at[h, slot], dev(x, zr(2 * step), q))
        for d in (1, -1):
            arrived(mine(h, zr(d), hi), b1_s.at[h, d % 8], b1_r.at[h, d % 8])
        for d in (1, -1, 2, -2):
            cross(h, d)

    def high_third(h):
        for d in (3, -3):
            arrived(mine(h, zr(d), hi), b1_s.at[h, d % 8], b1_r.at[h, d % 8])
            cross(h, d)
        for i, slot in enumerate((4, 0)):
            arrived(mine(h, zr(4), far(i)), b1_s.at[h, slot], b1_r.at[h, slot])
        cross(h, 4)

    def low_z(h, r, s):
        for i, step in enumerate((1, -1)):
            if r == 4 and s != i:
                continue
            ref = group(h, zr(-step * (r - 1)), s)
            send(ref, ref, a2_s.at[h, r - 1, i, s], a2_r.at[h, r - 1, i, s], dev(x, zr(step), q))

    def low_z_wait(h, r, s):
        for i, step in enumerate((1, -1)):
            if r == 4 and s != i:
                continue
            arrived(group(h, zr(-step * r), s), a2_s.at[h, r - 1, i, s], a2_r.at[h, r - 1, i, s])

    def begin(h):
        @pl.when(q == z)
        def _():
            keep_own(h).wait()

        @pl.when(q != z)
        def _():
            arrived(m.at[h, z // 2, x, q, z % 2], sc_s.at[h, 0], sc_r.at[h, q])

        for d in range(1, 8):
            arrived(m.at[h, z // 2, x, qr(d), z % 2], sc_s.at[h, d], sc_r.at[h, qr(d)])

    def first_sends(h):
        for d in (1, 3, 2):
            ref = mine(h, z, lo)
            send(ref, ref, a1_s.at[h, d - 1], a1_r.at[h, d - 1], dev(xr(d), z, q))
        high_first(h)
        cross(h, 0)

    def low_start(h):
        for d in (1, 3, 2):
            arrived(m.at[h, z // 2, xr(-d), lo, z % 2], a1_s.at[h, d - 1], a1_r.at[h, d - 1])
        for s in range(2):
            low_z(h, 1, s)

    def jump(h, origin, r, s):
        for i, step in enumerate((1, -1)):
            if r == 4 and s != i:
                continue
            ref = group(h, zr(-step * origin), s)
            target = dev(x, zr(step * (r - origin)), q)
            send(ref, ref, a2_s.at[h, r - 1, i, s], a2_r.at[h, r - 1, i, s], target)

    def low_far(h):
        for s in range(2):
            low_z_wait(h, 2, s)
            jump(h, 2, 3, s)
            jump(h, 2, 4, s)

    def low_rest(h):
        for r in (1, 3, 4):
            for s in range(2):
                low_z_wait(h, r, s)

    def low(h, r):
        for s in range(2):
            low_z_wait(h, r, s)
            if r < 4:
                low_z(h, r + 1, s)

    def hop(h, *offsets):
        for d in offsets:
            zz = zr(d)
            slot = d % 8
            arrived(at_x(h, zz, xr(-1)), b2_s.at[h, slot, 0], b2_r.at[h, slot, 0])
            arrived(at_x(h, zz, xr(1)), b2_s.at[h, slot, 1], b2_r.at[h, slot, 1])
            if d in (0, 1, 2, -3):
                ref = at_x(h, zz, xr(-1))
                send(ref, ref, b3_s.at[h, slot], b3_r.at[h, slot], dev(xr(1), z, q))
            else:
                ref = at_x(h, zz, xr(1))
                send(ref, ref, b3_s.at[h, slot], b3_r.at[h, slot], dev(xr(3), z, q))

    def hop_wait(h):
        for d in range(8):
            arrived(at_x(h, zr(d), xr(2)), b3_s.at[h, d], b3_r.at[h, d])

    def pair_copy(h, a):
        return remote(
            prod.at[h, a, :, 1 - core],
            r1.at[h, a],
            r1_s.at[h, a],
            r1_r.at[h, a],
            dev(x, z, q + 1 - 2 * core),
        )

    def y_copy(h, d, a):
        yy = (y + d) % NY
        return remote(
            prod.at[h, a, yy, core],
            r2.at[h, d - 1, a],
            r2_s.at[h, d - 1, a],
            r2_r.at[h, d - 1, a],
            dev(x, z, yy * 2 + core),
        )

    def multiply(h):
        def rows(a, _):
            weights = m[h].reshape(16 * W, W)
            part = jnp.dot(
                abf[pl.ds(pl.multiple_of(a * W, W), W), :], weights, preferred_element_type=F32
            )
            prod[h, a] = part.reshape(4, 2, 32, W)
            pair_copy(h, a).start()
            return 0

        lax.fori_loop(0, 4, rows, 0)

    last = ((z + 4) % NZ) // 2

    def part_product(a, k, h):
        left = abf[pl.ds(pl.multiple_of(a * W, W), W), pl.ds(pl.multiple_of(k * 1024, 1024), 1024)]
        return jnp.dot(left, m[h, k].reshape(4 * W, W), preferred_element_type=F32)

    def multiply_early(h):
        def rows(a, _):
            total = part_product(a, (last + 1) % 4, h)
            for d in (2, 3):
                total = total + part_product(a, (last + d) % 4, h)
            prod[h, a] = total.reshape(4, 2, 32, W)
            return 0

        lax.fori_loop(0, 4, rows, 0)

    def multiply_last(h):
        def rows(a, _):
            prod[h, a] = prod[h, a] + part_product(a, last, h).reshape(4, 2, 32, W)
            pair_copy(h, a).start()
            return 0

        lax.fori_loop(0, 4, rows, 0)

    def pair_sum(h):
        def rows(a, _):
            pair_copy(h, a).wait_recv()
            for yy in range(4):
                prod[h, a, yy, core] = prod[h, a, yy, core] + r1[h, a, yy]
            for d in (2, 1, 3):
                y_copy(h, d, a).start()
            return 0

        lax.fori_loop(0, 4, rows, 0)

    def row_part(h, a):
        total = prod[h, a, y, core]
        for d in (1, 2, 3):
            y_copy(h, d, a).wait_recv()
            total = total + r2[h, d - 1, a]
        return total

    outs = []

    def put(src, dst, i):
        copy = pltpu.make_async_copy(src, dst, out_sem.at[i])
        copy.start()
        outs.append(copy)

    def finish_first():
        for a in range(4):
            fc[a] = (-row_part(0, a) * flag1[a]).astype(BF16)
        put(fc, fc_out, 0)

    def finish_second():
        for a in range(4):
            bridge = jnp.dot(fc[a], top[...], preferred_element_type=F32)
            sc[a] = (-(row_part(1, a) + bridge) * flag2[a]).astype(BF16)
        put(sc, sc_out, 1)

    def share_rows():
        for d in range(1, 8):
            send(lm.at[1], mb.at[:, q], mb_s.at[d - 1], mb_r.at[d - 1], dev(x, z, qr(d)))
        for a in range(4):
            mb[a, q] = lm[1, a]

    def turn_rows():
        for d in range(1, 8):
            arrived(mb.at[:, qr(-d)], mb_s.at[d - 1], mb_r.at[d - 1])
        for a in range(4):
            mbt[a] = mb[a].reshape(W, W).T

    spot = x * NY + y
    others = [(dx, dy) for dx in range(NX) for dy in range(NY) if dx or dy]

    def plane(dx, dy):
        xx, yy = (x + dx) % NX, (y + dy) % NY
        return xx * NY + yy, dev(xx, z, yy * 2 + core)

    half = pl.ds(pl.multiple_of((1 - core) * 128, 128), 128)

    def swap_inverse():
        send(g.at[half], dz, p_s.at[78], p_r.at[78], dev(x, z, q + 1 - 2 * core))

    def inverse_rows(k):
        own = g[pl.ds(pl.multiple_of((core * 16 + spot) * 8, 8), 8), :]
        other = dz[pl.ds(pl.multiple_of(spot * 8, 8), 8), :]
        return jnp.where(z == 0, jnp.where(core == k, own, other), 0.0)

    def all_reduce(base, t, w0, u, w1, w3, w4, wf, enter):
        def sems(i):
            return p_s.at[base + i], p_r.at[base + i]

        twin = dev(x, z, q + 1 - 2 * core)
        send(t.at[1 - core], w0, *sems(0), twin)
        yield
        arrived(w0, *sems(0))
        u[...] = t[core] + w0[...]
        for i, (dx, dy) in enumerate(others):
            there, target = plane(dx, dy)
            send(u.at[there], w1.at[i], *sems(1 + i), target)
        yield
        total = u[spot]
        for i in range(15):
            arrived(w1.at[i], *sems(1 + i))
            total = total + w1[i]
        enter(w3, total)
        for d in range(1, 8):
            send(w3.at[z], w3.at[z], *sems(15 + d), dev(x, zr(d), q))
        yield
        for d in range(1, 8):
            arrived(w3.at[zr(-d)], *sems(15 + d))
        total = w3[0]
        for zz in range(1, 8):
            total = total + w3[zz]
        w4[spot] = total
        for i, (dx, dy) in enumerate(others):
            send(w4.at[spot], w4.at[spot], *sems(23 + i), plane(dx, dy)[1])
        yield
        for i, (dx, dy) in enumerate(others):
            arrived(w4.at[plane(-dx, -dy)[0]], *sems(23 + i))
        send(w4, wf.at[core], *sems(38), twin)
        wf[core] = w4[...]
        yield
        arrived(wf.at[1 - core], *sems(38))
        yield

    def enter_a(w3, total):
        w3[z, 0] = total[0] + inverse_rows(0)
        w3[z, 1] = total[1]

    def enter_b(w3, total):
        w3[z, 0] = total[0] - inverse_rows(1)

    reduce_a = all_reduce(0, ta, wa0, ua, wa1, wa3, wa4, waf, enter_a)
    reduce_b = all_reduce(39, tb, wb0, ub, wb1, wb3, wb4, wbf, enter_b)

    relayout(0)
    relayout(1)
    work(5)
    begin(0)
    first_sends(0)
    share_rows()
    relayout(2)
    begin(1)
    work(2)
    low_start(0)
    high_second(0)
    work(4)
    first_sends(1)
    relayout(3)
    work(3)
    low(0, 1)
    high_third(0)
    hop(0, 0, 1, -1, 2, -2)
    low_start(1)
    high_second(1)
    work(4)
    hop(0, 3, -3, 4)
    low(0, 2)
    low(0, 3)
    hop_wait(0)
    multiply_early(0)
    low(0, 4)
    multiply_last(0)
    low(1, 1)
    high_third(1)
    pair_sum(0)
    hop(1, 0, 1, -1, 2, -2)
    work(8)
    low(1, 2)
    hop(1, 3, -3, 4)
    work(8)
    turn_rows()
    low(1, 3)
    work(8)
    tops.wait()
    finish_first()
    first = fc[...].reshape(128, W)
    ta[:, :, 0] = contract(lm[0].reshape(128, W), first).reshape(2, 16, 8, W)
    ta[:, :, 1] = contract(first, lm[1].reshape(128, W)).reshape(2, 16, 8, W)
    next(reduce_a)
    hop_wait(1)
    next(reduce_a)
    multiply_early(1)
    low(1, 4)
    multiply_last(1)

    def second_term():
        total = jnp.zeros((W, W), F32)
        for a in range(4):
            for piece in split(prod[1, a].reshape(W, W)):
                total = total + jnp.dot(mbt[a], piece, preferred_element_type=F32)
        return total

    tb[...] = second_term().reshape(2, 16, 1, 8, W)
    next(reduce_b)
    work(1)
    next(reduce_b)
    work(40)
    swap_inverse()
    pair_sum(1)
    arrived(dz, p_s.at[78], p_r.at[78])
    next(reduce_a)
    next(reduce_b)
    next(reduce_a)
    next(reduce_b)
    next(reduce_a)
    finish_second()
    next(reduce_a)
    first_diag = -waf[:, :, 0].reshape(W, W)
    fd[...] = first_diag
    put(fd, fd_out, 2)
    cross_sum = waf[:, :, 1].reshape(W, W)
    lower = jnp.dot(first_diag.astype(BF16), top[...], preferred_element_type=F32)
    link[...] = (-(cross_sum + lower)).astype(BF16)
    put(link, link_out, 3)
    tail = -contract(top[...], link[...])
    for piece in split(cross_sum):
        tail = tail + contract(piece, top[...])
    next(reduce_b)
    next(reduce_b)
    sd[...] = wbf[:, :, 0].reshape(W, W) + tail
    put(sd, sd_out, 4)

    for copy in sent:
        copy.wait_send()

    for h in range(2):

        @pl.when(q != z)
        def _(h=h):
            spread(h, 0).wait_send()

        for d in range(1, 8):
            spread(h, d).wait_send()
        for a in range(4):
            pair_copy(h, a).wait_send()
            for d in (1, 2, 3):
                y_copy(h, d, a).wait_send()
    for copy in outs:
        copy.wait()


def hand_out(*refs):
    ins, outs, stage, sem = refs[:5], refs[5:10], refs[10:15], refs[15]
    loads = [pltpu.make_async_copy(ins[i], stage[i], sem.at[i]) for i in range(5)]
    stores = [pltpu.make_async_copy(stage[i], outs[i], sem.at[5 + i]) for i in range(5)]
    for copy in loads:
        copy.start()
    for load, store in zip(loads, stores):
        load.wait()
        store.start()
    for copy in stores:
        copy.wait()


def per_device(
    anc_inverse,
    first_lower,
    second_lower,
    second_top,
    struct_first,
    struct_keep,
    pivot_h,
    pivot_s,
    shifts,
    pole_index,
):
    hbm = pl.BlockSpec(memory_space=pl.ANY)
    dma = pltpu.SemaphoreType.DMA
    vmem = pltpu.VMEM
    shapes = (
        jax.ShapeDtypeStruct((4, 32, W), BF16),
        jax.ShapeDtypeStruct((W, W), F32),
        jax.ShapeDtypeStruct((W, W), BF16),
        jax.ShapeDtypeStruct((4, 32, W), BF16),
        jax.ShapeDtypeStruct((W, W), F32),
    )

    def reduce_scratch(count):
        return [
            vmem((2, 16, count, 8, W), F32),
            vmem((16, count, 8, W), F32),
            vmem((16, count, 8, W), F32),
            vmem((15, count, 8, W), F32),
            vmem((8, count, 8, W), F32),
            vmem((16, count, 8, W), F32),
            vmem((2, 16, count, 8, W), F32),
        ]

    results = pl.pallas_call(
        body,
        out_shape=shapes,
        in_specs=[hbm] * 10,
        out_specs=(hbm,) * 5,
        scratch_shapes=[
            vmem((4, 4096, W), BF16),
            vmem((2, 4096, 128), F32),
            vmem((1024, 4096), BF16),
            vmem((2, 4, 4, 8, 2, 16, W), BF16),
            vmem((2, 4, 32, W), BF16),
            vmem((2, 4, 32, W), BF16),
            vmem((4, 8, 32, W), BF16),
            vmem((4, W, W), BF16),
            vmem((2, 4, 4, 2, 32, W), F32),
            vmem((2, 4, 4, 32, W), F32),
            vmem((2, 3, 4, 32, W), F32),
            vmem((W, W), F32),
            vmem((W, W), F32),
            vmem((BLK, 128), F32),
            vmem((128, W), F32),
            vmem((4, 32, W), BF16),
            vmem((4, 32, W), BF16),
            vmem((W, W), F32),
            vmem((W, W), BF16),
            vmem((W, W), F32),
            vmem((W, W), BF16),
            pltpu.SMEM((128,), jnp.int32),
            pltpu.SMEM((128,), jnp.int32),
            pltpu.SMEM((40,), F32),
            pltpu.SMEM((40,), jnp.int32),
        ]
        + reduce_scratch(2)
        + reduce_scratch(1)
        + [
            dma((13,)),
            dma((5,)),
            dma((2, 8)),
            dma((2, 8)),
            dma((2,)),
            dma((7,)),
            dma((7,)),
            dma((2, 3)),
            dma((2, 3)),
            dma((2, 4, 2, 2)),
            dma((2, 4, 2, 2)),
            dma((2, 8)),
            dma((2, 8)),
            dma((2, 8, 2)),
            dma((2, 8, 2)),
            dma((2, 8)),
            dma((2, 8)),
            dma((2, 4)),
            dma((2, 4)),
            dma((2, 3, 4)),
            dma((2, 3, 4)),
            dma((79,)),
            dma((79,)),
        ],
        compiler_params=pltpu.CompilerParams(
            collective_id=0, has_side_effects=True, vmem_limit_bytes=62 * 1024 * 1024
        ),
        name="selected_inversion",
    )(
        anc_inverse.reshape(4, 4096, W),
        first_lower.reshape(4, 32, W),
        second_lower.reshape(4, 32, W),
        second_top,
        struct_first,
        struct_keep,
        pivot_h,
        pivot_s,
        shifts,
        pole_index,
    )
    fc, fd, link, sc, sd = pl.pallas_call(
        hand_out,
        out_shape=shapes,
        in_specs=[hbm] * 5,
        out_specs=(hbm,) * 5,
        scratch_shapes=[vmem(s.shape, s.dtype) for s in shapes] + [dma((10,))],
        name="outputs",
    )(*results)
    return fc[:, None], fd, link, sc[:, None], sd


def solution(mesh):
    return jax.shard_map(
        per_device,
        mesh=mesh,
        in_specs=(
            P(None, "prow", None, None, "pcol", None),
            P(None, "prow", "pcol", None),
            P(None, "prow", "pcol", None),
            P(),
            P(),
            P(),
            P(),
            P(),
            P(),
            P(),
        ),
        out_specs=(P(None, "prow", "pcol", None), P(), P(), P(None, "prow", "pcol", None), P()),
        check_vma=False,
    )
```
